32 devices in a mesh: dp: 8 (over z, x), tensor: 4 (over y, core).
Axes of the slice: x: 2, y: 2, z: 4, core: 2. Of those that a mesh axis runs over, the one named last changes fastest.
Arguments:
- layer_input: bfloat16 [32768, 768], P(('dp', 'tensor')), may hold values from -6 to 6
- out_cotangent: bfloat16 [32768, 768], P(('dp', 'tensor')), may hold values from -6 to 6
- teacher: bfloat16 [32768, 768], P(('dp', 'tensor')), may hold values from -6 to 6
- valid_mask: int32 [8, 2048], P('dp'), may hold values from 0 to 1, as said below
- prompt_docs: int32 [8, 2048], P('dp'), may hold values from 0 to 3, never falling along the last dimension, each value on 1 to 1024 neighbouring positions
- pass_embed: float32 [768], replicated, may hold values from -1.75 to 1.75
- first_gain: float32 [768], replicated, may hold values from 0.5 to 1.5
- first_shift: float32 [768], replicated, may hold values from -1.75 to 1.75
- project_in: bfloat16 [768, 3, 768], P(None, None, 'tensor'), may hold values from -0.3125 to 0.3125
- project_out: bfloat16 [768, 768], P('tensor'), may hold values from -1.25 to 1.25
- second_gain: float32 [768], replicated, may hold values from 0.5 to 1.5
- second_shift: float32 [768], replicated, may hold values from -1.75 to 1.75
- expand_weight: bfloat16 [768, 3072], P(None, 'tensor'), may hold values from -0.21875 to 0.21875
- reduce_weight: bfloat16 [3072, 768], P('tensor'), may hold values from -0.109375 to 0.109375
Outputs:
- layer_output: bfloat16 [32768, 768], P(('dp', 'tensor'))
- loss: float32 [], replicated
- input_gradient: bfloat16 [32768, 768], P(('dp', 'tensor'))
- embed_gradient: float32 [768], replicated
- first_gain_gradient: float32 [768], replicated
- first_shift_gradient: float32 [768], replicated
- project_in_gradient: float32 [768, 3, 768], P(None, None, 'tensor')
- project_out_gradient: float32 [768, 768], P('tensor')
- second_gain_gradient: float32 [768], replicated
- second_shift_gradient: float32 [768], replicated
- expand_gradient: float32 [768, 3072], P(None, 'tensor')
- reduce_gradient: float32 [3072, 768], P('tensor')
The draws below stay inside these ranges and needn't reach their ends.
Inputs may be any that keep to these rules, and one draw needn't show every extreme that they name: `valid_mask`: 1 marks a valid continuation token, 0 a padded one; the first token of every continuation is valid. `prompt_docs`: document number of each prompt token of its group; never falls along the prompt; each document has at most 1024 tokens.
All inputs are finite; a program needn't handle non-finite values.
Results may differ from the reference program's by a relative error of at most 0.017.
The reference program's roundings to bfloat16 on the way count: a program that leaves them out, or rounds other values in their place, can miss the bound.
Values may be sent and summed in bfloat16 or wider, within the bound.
No kernel may reach another device: no remote copies, remote signals or barrier semaphores. Data moves between devices by JAX's collectives and lax.ppermute only.
A program may use at most 448 MiB of HBM per device.

```python
import math
import jax
import jax.numpy as jnp
import numpy as np
from jax import lax

D = 768
H = 12
FF = 3072
PROMPT = 2048
CONT = 256
CONTS = 8
SEGS = 4
GLEN = 4096
GROUPS = 8
TOKENS = 32768


def draw_valid_mask(key, part):
    width = CONTS * CONT
    group_ids = jnp.arange(GROUPS, dtype=jnp.int32)
    limits = 300 + 600 * group_ids // max(GROUPS - 1, 1)
    rolls = jax.random.randint(key, (GROUPS, width), 0, 1000, dtype=jnp.int32)
    starts = jnp.arange(width, dtype=jnp.int32) % CONT == 0
    keeper = (rolls < limits[:, None]) | starts[None, :]
    return keeper.astype(jnp.int32)


def steps_of(stream_key, extent, cuts, least, largest):
    gain, own = 1.0, jax.random.fold_in(stream_key, 6)
    for dim, parts in cuts:
        heights = jnp.exp(jax.random.uniform(jax.random.fold_in(own, dim), (parts,), jnp.float32, least / len(cuts), largest / len(cuts)))
        gain = gain * jnp.repeat(heights, extent[dim] // parts).reshape([-1 if axis == dim else 1 for axis in range(len(extent))])
    return gain


def split_up(number_of, total, limit, lean):
    weights = [(1 << 20) // math.isqrt(rank ** lean) + 1 for rank in range(2, number_of + 1)]
    surplus, holding = total - limit - (number_of - 1), [1] * (number_of - 1)
    while surplus > 0:
        free = [i for i in range(number_of - 1) if holding[i] < limit]
        pool, remaining = sum([weights[i] for i in free]), surplus
        for i in free:
            addition = min(limit - holding[i], max(1, remaining * weights[i] // pool), surplus)
            holding[i] = holding[i] + addition
            surplus = surplus - addition
    return np.array([limit] + holding)


def uneven(own_key, number_of, total, bound, lean):
    if number_of == 2:
        one = jax.random.randint(own_key, (), max(1, total - bound), min(bound, total - 1) + 1)
        return jnp.stack([one, total - one])
    tallies = jnp.asarray(split_up(number_of, total, bound, lean), jnp.int32)
    pairs = (number_of - 1) // 2
    source_of, taker = tallies[1:1 + 2 * pairs:2], tallies[2:2 + 2 * pairs:2]
    slack = jnp.minimum(source_of - 1, bound - taker)
    moved = jax.random.randint(jax.random.fold_in(own_key, 1), (pairs,), 0, 1 << 20) % (slack + 1)
    tallies = tallies.at[1:1 + 2 * pairs:2].set(source_of - moved).at[2:2 + 2 * pairs:2].set(taker + moved)
    return tallies[jax.random.permutation(jax.random.fold_in(own_key, 2), number_of)]


def noise(own_key, extent, scale, reach, cuts=(), held_as=jnp.bfloat16):
    loudness = steps_of(own_key, extent, cuts, -0.22, 0.18) if cuts else 1.0
    array = jax.random.normal(own_key, extent, jnp.float32) * scale * loudness
    return jnp.minimum(jnp.maximum(array, -reach), reach).astype(held_as)


def setup_inputs(seed: int = 0) -> dict:
    streams_of = jax.random.split(jax.random.key(seed), 15)
    return {
        "layer_input": noise(streams_of[0], (TOKENS, D), 1.0, 6.0, ((0, 32),)),
        "out_cotangent": noise(streams_of[1], (TOKENS, D), 1.0, 6.0, ((0, 32),)),
        "teacher": noise(streams_of[2], (TOKENS, D), 1.0, 6.0, ((0, 32),)),
        "valid_mask": draw_valid_mask(jax.random.fold_in(streams_of[14], 71), 0),
        "prompt_docs": jax.vmap(lambda own: jnp.searchsorted(jnp.cumsum(uneven(own, SEGS, PROMPT, PROMPT // 2, 0)), jnp.arange(PROMPT), side="right"))(jax.random.split(streams_of[4], GROUPS)).reshape((GROUPS, PROMPT)).astype(jnp.int32),
        "pass_embed": noise(streams_of[5], (D,), 0.3, 1.75, (), jnp.float32),
        "first_gain": jnp.clip(1.0 + 0.1 * jax.random.normal(streams_of[6], (D,), jnp.float32), 0.5, 1.5),
        "first_shift": noise(streams_of[7], (D,), 0.3, 1.75, (), jnp.float32),
        "project_in": noise(streams_of[8], (D, 3, D), (D // 2) ** -0.5, 0.3125, ((2, 4),)),
        "project_out": noise(streams_of[9], (D, D), (D // 32) ** -0.5, 1.25, ((0, 4),)),
        "second_gain": jnp.clip(1.0 + 0.1 * jax.random.normal(streams_of[10], (D,), jnp.float32), 0.5, 1.5),
        "second_shift": noise(streams_of[11], (D,), 0.3, 1.75, (), jnp.float32),
        "expand_weight": noise(streams_of[12], (D, FF), D ** -0.5, 0.21875, ((1, 4),)),
        "reduce_weight": noise(streams_of[13], (FF, D), FF ** -0.5, 0.109375, ((0, 4),)),
    }


@jax.custom_vjp
def low(v):
    return lax.optimization_barrier(v.astype(jnp.bfloat16)).astype(jnp.float32)

@jax.custom_vjp
def low_back(v):
    return v

def low_keep(v):
    return (low(v), None)

def low_pass(kept, grad):
    return (grad,)

def back_keep(v):
    return (v, None)

def back_low(kept, grad):
    return (low(grad),)
low.defvjp(low_keep, low_pass)
low_back.defvjp(back_keep, back_low)
norm_eps = 1e-05
highest = lax.Precision.HIGHEST

def normalize(values):
    centred = values - lax.optimization_barrier(jnp.mean(values, axis=-1, keepdims=True))
    spread = lax.optimization_barrier(jnp.mean(centred * centred, axis=-1, keepdims=True))
    return centred * lax.rsqrt(spread + norm_eps)

def group_attention(queries, key_rows, value_rows, doc_ids, valid_ids):
    block_rows = min(512, GLEN)
    head_dim = D // H
    score_scale = head_dim ** (-0.5)
    col_ids = jnp.arange(GLEN, dtype=jnp.int32)
    prompt_cols = col_ids < PROMPT
    full_docs = jnp.concatenate([doc_ids, jnp.full((GLEN - PROMPT,), -1, jnp.int32)])
    full_valid = jnp.concatenate([jnp.ones((PROMPT,), jnp.int32), valid_ids])
    part_ids = jnp.where(prompt_cols, -1, (col_ids - PROMPT) // CONT).astype(jnp.int32)

    def one_block(block_begin):
        row_ids = block_begin + jnp.arange(block_rows, dtype=jnp.int32)
        row_docs = lax.dynamic_slice_in_dim(full_docs, block_begin, block_rows)
        row_parts = lax.dynamic_slice_in_dim(part_ids, block_begin, block_rows)
        causal = col_ids[None, :] <= row_ids[:, None]
        in_prompt = (row_ids < PROMPT)[:, None]
        prompt_ok = prompt_cols[None, :] & causal & (full_docs[None, :] == row_docs[:, None])
        tail_ok = prompt_cols[None, :] | causal & (part_ids[None, :] == row_parts[:, None]) & (full_valid[None, :] == 1)
        allowed = jnp.where(in_prompt, prompt_ok, tail_ok)
        block_queries = lax.dynamic_slice_in_dim(queries, block_begin, block_rows)
        raw_scores = jnp.einsum('qhd,khd->hqk', block_queries, key_rows, precision=highest)
        scores = low_back(raw_scores * score_scale)
        scores = jnp.where(allowed[None], scores, -jnp.inf)
        maxima = lax.optimization_barrier(jnp.max(scores, axis=-1, keepdims=True))
        exponent = jnp.exp(scores - maxima)
        attn_probs = exponent / lax.optimization_barrier(jnp.sum(exponent, axis=-1, keepdims=True))
        return jnp.einsum('hqk,khd->qhd', low(attn_probs), value_rows, precision=highest)
    begins = jnp.arange(0, GLEN, block_rows, dtype=jnp.int32)
    outputs = lax.map(jax.checkpoint(one_block), begins)
    return outputs.reshape(GLEN, H, head_dim)

def group_forward(params, inputs):
    pass_embed, first_gain, first_shift, project_in, project_out, second_gain, second_shift, expand_weight, reduce_weight = params
    group_input, group_teacher, doc_ids, valid_ids = inputs
    head_dim = D // H
    hidden_in = group_input + pass_embed
    first_norm = low(normalize(hidden_in) * first_gain + first_shift)
    projected = jnp.dot(first_norm, project_in.reshape(D, 3 * D), precision=highest)
    projected = low(low_back(projected))
    queries = projected[:, :D].reshape(GLEN, H, head_dim)
    key_rows = projected[:, D:2 * D].reshape(GLEN, H, head_dim)
    value_rows = projected[:, 2 * D:].reshape(GLEN, H, head_dim)
    attended = group_attention(queries, key_rows, value_rows, doc_ids, valid_ids).reshape(GLEN, D)
    attended = low(low_back(attended))
    attn_branch = low_back(jnp.dot(attended, project_out, precision=highest))
    middle = hidden_in + attn_branch
    second_norm = low(normalize(middle) * second_gain + second_shift)
    pre_act = low_back(jnp.dot(second_norm, expand_weight, precision=highest))
    activated = low(jax.nn.gelu(pre_act, approximate=True))
    mlp_branch = low_back(jnp.dot(activated, reduce_weight, precision=highest))
    layer_out = middle + mlp_branch
    row_valid = jnp.concatenate([jnp.zeros((PROMPT,), jnp.float32), valid_ids.astype(jnp.float32)])
    deviation = layer_out - group_teacher
    squares = jnp.sum(row_valid[:, None] * deviation * deviation)
    return (layer_out, squares)

def forward(params, stacked_input, stacked_teacher, doc_ids, valid_ids, divisor):

    def step(total, inputs):
        layer_out, squares = group_forward(params, inputs)
        return (total + squares, layer_out)
    total, outputs = lax.scan(jax.checkpoint(step), jnp.zeros((), jnp.float32), (stacked_input, stacked_teacher, doc_ids, valid_ids))
    return (outputs, total / divisor)

def reference(layer_input, out_cotangent, teacher, valid_mask, prompt_docs, pass_embed, first_gain, first_shift, project_in, project_out, second_gain, second_shift, expand_weight, reduce_weight):
    stacked_input = layer_input.astype(jnp.float32).reshape(GROUPS, GLEN, D)
    stacked_teacher = teacher.astype(jnp.float32).reshape(GROUPS, GLEN, D)
    divisor = jnp.sum(valid_mask).astype(jnp.float32) * D
    params = (pass_embed, first_gain, first_shift, project_in.astype(jnp.float32), project_out.astype(jnp.float32), second_gain, second_shift, expand_weight.astype(jnp.float32), reduce_weight.astype(jnp.float32))

    def objective(inputs_f, params_f):
        return forward(params_f, inputs_f, stacked_teacher, prompt_docs, valid_mask, divisor)
    (outputs, loss), pull = jax.vjp(objective, stacked_input, params)
    input_adj, param_adj = pull((out_cotangent.astype(jnp.float32).reshape(GROUPS, GLEN, D), jnp.ones((), jnp.float32)))
    return (outputs.reshape(TOKENS, D).astype(jnp.bfloat16), loss, input_adj.reshape(TOKENS, D).astype(jnp.bfloat16), param_adj[0], param_adj[1], param_adj[2], param_adj[3], param_adj[4], param_adj[5], param_adj[6], param_adj[7], param_adj[8])
```

```python
import functools

import jax
import jax.numpy as jnp
from jax import lax
from jax.experimental import pallas as pl
from jax.experimental.pallas import tpu as pltpu
from jax.sharding import PartitionSpec as P

D = 768
H = 12
HD = D // H
PROMPT = 2048
CONT = 256
CONTS = 8
GLEN = 4096
DOC_MAX = 1024
NEG = -1e30
SCALE = HD ** (-0.5)
norm_eps = 1e-05
bf16 = jnp.bfloat16
f32 = jnp.float32


def dot_f32(a, b):
    return jnp.dot(a, b, preferred_element_type=f32)


def fwd_kernel(q_ref, k_ref, v_ref, start_ref, bias_ref, o_ref, wide_ref, lse_ref, keys_ref):
    keys_ref[...] = k_ref[0].T

    def finish(off, top, total, acc):
        out = acc / total
        wide_ref[0, :, pl.ds(off, CONT)] = out
        o_ref[0, :, pl.ds(off, CONT)] = out.astype(bf16)
        lse_ref[0, :, pl.ds(off, CONT)] = top + jnp.log(total)

    causal = lax.broadcasted_iota(jnp.int32, (CONT, CONT), 0) <= lax.broadcasted_iota(
        jnp.int32, (CONT, CONT), 1
    )

    def continuation(c, carry):
        off = pl.multiple_of(PROMPT + c * CONT, CONT)
        queries = q_ref[0, :, pl.ds(off, CONT)]
        s1 = dot_f32(keys_ref[0:PROMPT, :], queries)
        s2 = dot_f32(keys_ref[pl.ds(off, CONT), :], queries)
        bias = bias_ref[pl.ds(pl.multiple_of(c * CONT, CONT), CONT), :]
        s2 = jnp.where(causal, s2 + jnp.concatenate([bias, bias], 1), NEG)
        top = jnp.maximum(jnp.max(s1, 0, keepdims=True), jnp.max(s2, 0, keepdims=True))
        p1 = jnp.exp(s1 - top)
        p2 = jnp.exp(s2 - top)
        total = jnp.sum(p1, 0, keepdims=True) + jnp.sum(p2, 0, keepdims=True)
        acc = dot_f32(v_ref[0, :, 0:PROMPT], p1.astype(bf16))
        acc = acc + dot_f32(v_ref[0, :, pl.ds(off, CONT)], p2.astype(bf16))
        finish(off, top, total, acc)
        return carry

    lax.fori_loop(0, CONTS, continuation, 0)
    for off in range(0, PROMPT, CONT):
        low = max(0, off - DOC_MAX)
        span = off + CONT - low
        s = dot_f32(keys_ref[low : off + CONT, :], q_ref[0, :, off : off + CONT])
        key_ids = low + lax.broadcasted_iota(jnp.int32, (span, CONT), 0)
        row_ids = off + lax.broadcasted_iota(jnp.int32, (span, CONT), 1)
        s = jnp.where((key_ids <= row_ids) & (key_ids >= start_ref[:, off : off + CONT]), s, NEG)
        top = jnp.max(s, 0, keepdims=True)
        p = jnp.exp(s - top)
        finish(off, top, jnp.sum(p, 0, keepdims=True), dot_f32(v_ref[0, :, low : off + CONT], p.astype(bf16)))


def head_spec(shift, heads):
    return pl.BlockSpec((1, HD, GLEN), lambda h: (h + shift * heads, 0, 0))


def attn_fwd(qkv, doc_start, key_bias):
    heads = qkv.shape[0] // 3
    return pl.pallas_call(
        fwd_kernel,
        grid=(heads,),
        in_specs=[
            head_spec(0, heads),
            head_spec(1, heads),
            head_spec(2, heads),
            pl.BlockSpec((1, PROMPT), lambda h: (0, 0)),
            pl.BlockSpec((GLEN - PROMPT, 128), lambda h: (0, 0)),
        ],
        out_specs=[
            head_spec(0, heads),
            head_spec(0, heads),
            pl.BlockSpec((1, 1, GLEN), lambda h: (h, 0, 0)),
        ],
        out_shape=[
            jax.ShapeDtypeStruct((heads, HD, GLEN), bf16),
            jax.ShapeDtypeStruct((heads, HD, GLEN), f32),
            jax.ShapeDtypeStruct((heads, 1, GLEN), f32),
        ],
        scratch_shapes=[pltpu.VMEM((GLEN, HD), bf16)],
        name="attn_fwd",
    )(qkv, qkv, qkv, doc_start, key_bias)


KEYS = 512
SPAN = 512


def bwd_kernel(
    q_ref, k_ref, v_ref, g_ref, wide_ref, lse_ref, start_ref, bias_ref,
    dq_ref, dk_ref, dv_ref, qn, kn, vn, gn, inner, dq,
):
    qn[...] = q_ref[0].T
    kn[...] = k_ref[0].T
    vn[...] = v_ref[0].T
    gn[...] = g_ref[0].T
    inner[...] = jnp.sum(g_ref[0].astype(f32) * wide_ref[0], 0, keepdims=True)
    dq[...] = jnp.zeros_like(dq)

    def block(key_off, key_span, off, span, mask):
        rows = pl.ds(off, span)
        keys = pl.ds(key_off, key_span)
        s = dot_f32(kn[keys, :], q_ref[0, :, rows])
        if mask is not None:
            s = mask(s)
        p = jnp.exp(s - lse_ref[0, :, rows])
        dp = dot_f32(vn[keys, :], g_ref[0, :, rows])
        ds = (p * (dp - inner[:, rows])).astype(bf16)
        dv = dot_f32(p.astype(bf16), gn[rows, :])
        dk = dot_f32(ds, qn[rows, :])
        dq[:, rows] += dot_f32(k_ref[0, :, keys], ds)
        return dk, dv

    def emit(key_off, key_span, dk, dv):
        dk_ref[0, :, pl.ds(key_off, key_span)] = dk.T.astype(bf16)
        dv_ref[0, :, pl.ds(key_off, key_span)] = dv.T.astype(bf16)

    def key_block(b, carry):
        key_off = pl.multiple_of(b * KEYS, KEYS)

        def continuation(c, acc):
            off = pl.multiple_of(PROMPT + c * SPAN, SPAN)
            dk, dv = block(key_off, KEYS, off, SPAN, None)
            return acc[0] + dk, acc[1] + dv

        zero = jnp.zeros((KEYS, HD), f32)
        acc = lax.fori_loop(0, (GLEN - PROMPT) // SPAN, continuation, (zero, zero))

        def prompt(i, acc):
            off = pl.multiple_of(i * CONT, CONT)

            def mask(s):
                key_ids = key_off + lax.broadcasted_iota(jnp.int32, s.shape, 0)
                row_ids = off + lax.broadcasted_iota(jnp.int32, s.shape, 1)
                keep = (key_ids <= row_ids) & (key_ids >= start_ref[:, pl.ds(off, CONT)])
                return jnp.where(keep, s, NEG)

            dk, dv = block(key_off, KEYS, off, CONT, mask)
            return acc[0] + dk, acc[1] + dv

        last = jnp.minimum((key_off + KEYS + DOC_MAX - 2) // CONT + 1, PROMPT // CONT)
        acc = lax.fori_loop(key_off // CONT, last, prompt, acc)
        emit(key_off, KEYS, *acc)
        return carry

    lax.fori_loop(0, PROMPT // KEYS, key_block, 0)
    causal = lax.broadcasted_iota(jnp.int32, (CONT, CONT), 0) <= lax.broadcasted_iota(
        jnp.int32, (CONT, CONT), 1
    )

    def own(c, carry):
        off = pl.multiple_of(PROMPT + c * CONT, CONT)
        bias = bias_ref[pl.ds(pl.multiple_of(c * CONT, CONT), CONT), :]

        def mask(s):
            return jnp.where(causal, s + jnp.concatenate([bias, bias], 1), NEG)

        emit(off, CONT, *block(off, CONT, off, CONT, mask))
        return carry

    lax.fori_loop(0, CONTS, own, 0)
    dq_ref[0] = (dq[...] * SCALE).astype(bf16)


def attn_bwd(qkv, adj, wide, lse, doc_start, key_bias):
    heads = qkv.shape[0] // 3
    shape = jax.ShapeDtypeStruct((heads, HD, GLEN), bf16)
    return pl.pallas_call(
        bwd_kernel,
        grid=(heads,),
        in_specs=[
            head_spec(0, heads),
            head_spec(1, heads),
            head_spec(2, heads),
            head_spec(0, heads),
            head_spec(0, heads),
            pl.BlockSpec((1, 1, GLEN), lambda h: (h, 0, 0)),
            pl.BlockSpec((1, PROMPT), lambda h: (0, 0)),
            pl.BlockSpec((GLEN - PROMPT, 128), lambda h: (0, 0)),
        ],
        out_specs=[head_spec(0, heads)] * 3,
        out_shape=[shape] * 3,
        scratch_shapes=[pltpu.VMEM((GLEN, HD), bf16)] * 4
        + [pltpu.VMEM((1, GLEN), f32), pltpu.VMEM((HD, GLEN), f32)],
        name="attn_bwd",
    )(qkv, qkv, qkv, adj, wide, lse, doc_start, key_bias)


def normalize(values):
    centred = values - jnp.mean(values, axis=-1, keepdims=True)
    spread = jnp.mean(centred * centred, axis=-1, keepdims=True)
    return centred * lax.rsqrt(spread + norm_eps)


def affine_norm(values, norm_gain, norm_shift):
    return normalize(values) * norm_gain + norm_shift


def tanh_gelu(values):
    return jax.nn.gelu(values, approximate=True)


def dot(a, b, ca, cb):
    return lax.dot_general(a, b, (((ca,), (cb,)), ((), ())), preferred_element_type=f32)


def swap(x, bit, axis="tensor"):
    size = lax.axis_size(axis)
    return lax.ppermute(x, axis, [(i, i ^ bit) for i in range(size)])


def butterfly(x, axis):
    bit = 1
    while bit < lax.axis_size(axis):
        x = x + swap(x, bit, axis)
        bit *= 2
    return x


def gather4(x):
    far = swap(x, 2)
    near = swap(x, 1)
    return [x, near, far, swap(far, 1)]


def scatter4(parts):
    near1 = swap(parts[1], 1)
    near3 = swap(parts[3], 1)
    across = (parts[2].astype(f32) + near3.astype(f32)).astype(bf16)
    mine = parts[0].astype(f32) + near1.astype(f32)
    return mine + swap(across, 2).astype(f32)


def shards(
    layer_input,
    out_cotangent,
    teacher,
    valid_mask,
    prompt_docs,
    pass_embed,
    first_gain,
    first_shift,
    project_in,
    project_out,
    second_gain,
    second_shift,
    expand_weight,
    reduce_weight,
):
    rows = layer_input.shape[0]
    width = project_out.shape[0]
    heads = width // HD
    t = lax.axis_index("tensor")
    slots = [t ^ k for k in range(4)]
    valid = valid_mask[0]
    docs = prompt_docs[0]
    valid_total = butterfly(jnp.sum(valid).astype(f32).reshape(1, 1), "dp")[0, 0]
    divisor = valid_total * D
    doc_start = jnp.zeros_like(docs)
    for v in range(3):
        doc_start = doc_start + jnp.where(docs > v, jnp.sum((docs == v).astype(jnp.int32)), 0)
    doc_start = doc_start[None, :]
    key_bias = jnp.broadcast_to(jnp.where(valid == 1, 0.0, NEG).astype(f32)[:, None], (GLEN - PROMPT, 128))
    row_valid = lax.dynamic_slice_in_dim(
        jnp.concatenate([jnp.zeros((PROMPT,), f32), valid.astype(f32)]), t * rows, rows
    )[:, None]

    hidden_in = layer_input.astype(f32) + pass_embed
    first_affine, first_pull = jax.vjp(affine_norm, hidden_in, first_gain, first_shift)
    first_blocks = gather4(first_affine.astype(bf16))
    in_matrix = project_in.reshape(D, 3 * width)

    expand_weight, reduce_weight, project_out, _ = lax.optimization_barrier(
        (expand_weight, reduce_weight, project_out, first_blocks[2])
    )
    out_blocks = gather4(project_out)
    expand_blocks = gather4(expand_weight)
    reduce_blocks = gather4(reduce_weight)
    out_full = jnp.concatenate(out_blocks, 0)

    qkv = jnp.zeros((3 * width, GLEN), bf16)
    for k in range(4):
        part = dot(in_matrix, first_blocks[k], 0, 1).astype(bf16)
        part = jnp.concatenate([part[:width] * SCALE, part[width:]], 0)
        qkv = lax.dynamic_update_slice(qkv, part, (0, slots[k] * rows))
    qkv = qkv.reshape(3 * heads, HD, GLEN)
    attended, attended_wide, logsum = attn_fwd(qkv, doc_start, key_bias)

    att = attended.reshape(width, GLEN)
    cuts = [lax.dynamic_slice(att, (0, slots[k] * rows), (width, rows)) for k in range(4)]
    att_own = jnp.concatenate([cuts[0]] + [swap(cuts[k], k) for k in (1, 2, 3)], 0)
    attn_branch = dot(att_own, out_full, 0, 0)
    middle = hidden_in + attn_branch
    second_affine, second_pull = jax.vjp(affine_norm, middle, second_gain, second_shift)
    second_norm = second_affine.astype(bf16)
    acts, pulls = [], []
    mlp_branch = 0.0
    for k in range(4):
        pre_act = dot(second_norm, expand_blocks[k], 1, 0)
        activated, pull = jax.vjp(tanh_gelu, pre_act)
        acts.append(activated.astype(bf16))
        pulls.append(pull)
        mlp_branch = mlp_branch + dot(acts[k], reduce_blocks[k], 1, 0)
    layer_out = middle + mlp_branch
    deviation = row_valid * (layer_out - teacher.astype(f32))
    squares_part = jnp.sum(deviation * deviation)
    out_adj = out_cotangent.astype(f32) + 2.0 / divisor * deviation
    branch_adj = out_adj.astype(bf16)
    second_adj = 0.0
    reduce_parts, expand_parts = [], []
    pre_adjs = []
    for k in range(4):
        act_adj = dot(branch_adj, reduce_blocks[k], 1, 1)
        pre_adjs.append(pulls[k](act_adj)[0].astype(bf16))
        second_adj = second_adj + dot(pre_adjs[k], expand_blocks[k], 1, 1)
    middle_part, second_gain_part, second_shift_part = second_pull(second_adj)
    middle_adj = out_adj + middle_part
    attn_adj = middle_adj.astype(bf16)
    att_adj = dot(out_full, attn_adj, 1, 1).astype(bf16)
    att_adj_full = jnp.zeros((width, GLEN), bf16)
    for k in range(4):
        piece = att_adj[k * width : (k + 1) * width]
        piece = swap(piece, k) if k else piece
        att_adj_full = lax.dynamic_update_slice(att_adj_full, piece, (0, slots[k] * rows))

    for k in range(4):
        reduce_parts.append(dot(acts[k], branch_adj, 0, 0).astype(bf16))
        expand_parts.append(dot(second_norm, pre_adjs[k], 0, 0).astype(bf16))
    out_parts = dot(att_own, attn_adj, 1, 0).astype(bf16)
    out_parts = [out_parts[k * width : (k + 1) * width] for k in range(4)]
    reduce_grad = scatter4(reduce_parts).astype(bf16)
    expand_grad = scatter4(expand_parts).astype(bf16)
    out_proj_grad = scatter4(out_parts).astype(bf16)
    reduce_grad, expand_grad, out_proj_grad = lax.psum((reduce_grad, expand_grad, out_proj_grad), "dp")

    dq, dk, dv = attn_bwd(qkv, att_adj_full.reshape(heads, HD, GLEN), attended_wide, logsum, doc_start, key_bias)
    proj_adj = jnp.concatenate([g.reshape(width, GLEN) for g in (dq, dk, dv)], 0)
    pieces = [lax.dynamic_slice(proj_adj, (0, slots[k] * rows), (3 * width, rows)) for k in range(4)]
    first_parts = [dot(pieces[k], in_matrix, 0, 1).astype(bf16) for k in range(4)]
    first_adj = scatter4(first_parts)
    in_proj_grad = 0.0
    for k in range(4):
        in_proj_grad = in_proj_grad + dot(first_blocks[k], pieces[k], 0, 1)
    in_proj_grad = lax.psum(in_proj_grad.astype(bf16), "dp")
    hidden_part, first_gain_part, first_shift_part = first_pull(first_adj)
    input_adj = middle_adj + hidden_part
    embed_part = jnp.sum(input_adj, axis=0)
    small = jnp.stack(
        [
            embed_part,
            first_gain_part,
            first_shift_part,
            second_gain_part,
            second_shift_part,
            jnp.full((D,), squares_part),
        ]
    )
    small = butterfly(butterfly(small, "tensor"), "dp")
    return (
        layer_out.astype(bf16),
        small[5, 0] / divisor,
        input_adj.astype(bf16),
        small[0],
        small[1],
        small[2],
        in_proj_grad.astype(f32).reshape(D, 3, width),
        out_proj_grad.astype(f32),
        small[3],
        small[4],
        expand_grad.astype(f32),
        reduce_grad.astype(f32),
    )


def solution(mesh):
    rows = P(("dp", "tensor"), None)
    return jax.shard_map(
        shards,
        mesh=mesh,
        in_specs=(
            rows,
            rows,
            rows,
            P("dp", None),
            P("dp", None),
            P(),
            P(),
            P(),
            P(None, None, "tensor"),
            P("tensor", None),
            P(),
            P(),
            P(None, "tensor"),
            P("tensor", None),
        ),
        out_specs=(
            rows,
            P(),
            rows,
            P(),
            P(),
            P(),
            P(None, None, "tensor"),
            P("tensor", None),
            P(),
            P(),
            P(None, "tensor"),
            P("tensor", None),
        ),
        check_vma=False,
    )
```

```python
import jax
import jax.numpy as jnp
from jax import lax
from jax.experimental import pallas as pl
from jax.experimental.pallas import tpu as pltpu
from jax.sharding import PartitionSpec as P


D = 768
H = 12
HD = D // H
PROMPT = 2048
CONT = 256
CONTS = 8
GLEN = 4096
DOC_MAX = 1024
NEG = -1e30
SCALE = HD ** (-0.5)
norm_eps = 1e-05
bf16 = jnp.bfloat16
f32 = jnp.float32


def dot_f32(a, b):
    return jnp.dot(a, b, preferred_element_type=f32)


def fwd_kernel(q_ref, k_ref, v_ref, start_ref, bias_ref, o_ref, wide_ref, lse_ref, keys_ref):
    keys_ref[...] = k_ref[0].T

    def finish(off, top, total, acc):
        out = acc / total
        wide_ref[0, :, pl.ds(off, CONT)] = out
        o_ref[0, :, pl.ds(off, CONT)] = out.astype(bf16)
        lse_ref[0, :, pl.ds(off, CONT)] = top + jnp.log(total)

    causal = lax.broadcasted_iota(jnp.int32, (CONT, CONT), 0) <= lax.broadcasted_iota(
        jnp.int32, (CONT, CONT), 1
    )

    def continuation(c, carry):
        off = pl.multiple_of(PROMPT + c * CONT, CONT)
        queries = q_ref[0, :, pl.ds(off, CONT)]
        s1 = dot_f32(keys_ref[0:PROMPT, :], queries)
        s2 = dot_f32(keys_ref[pl.ds(off, CONT), :], queries)
        bias = bias_ref[pl.ds(pl.multiple_of(c * CONT, CONT), CONT), :]
        s2 = jnp.where(causal, s2 + jnp.concatenate([bias, bias], 1), NEG)
        top = jnp.maximum(jnp.max(s1, 0, keepdims=True), jnp.max(s2, 0, keepdims=True))
        p1 = jnp.exp(s1 - top)
        p2 = jnp.exp(s2 - top)
        total = jnp.sum(p1, 0, keepdims=True) + jnp.sum(p2, 0, keepdims=True)
        acc = dot_f32(v_ref[0, :, 0:PROMPT], p1.astype(bf16))
        acc = acc + dot_f32(v_ref[0, :, pl.ds(off, CONT)], p2.astype(bf16))
        finish(off, top, total, acc)
        return carry

    lax.fori_loop(0, CONTS, continuation, 0)
    for off in range(0, PROMPT, CONT):
        low = max(0, off - DOC_MAX)
        span = off + CONT - low
        s = dot_f32(keys_ref[low : off + CONT, :], q_ref[0, :, off : off + CONT])
        key_ids = low + lax.broadcasted_iota(jnp.int32, (span, CONT), 0)
        row_ids = off + lax.broadcasted_iota(jnp.int32, (span, CONT), 1)
        s = jnp.where((key_ids <= row_ids) & (key_ids >= start_ref[:, off : off + CONT]), s, NEG)
        top = jnp.max(s, 0, keepdims=True)
        p = jnp.exp(s - top)
        finish(off, top, jnp.sum(p, 0, keepdims=True), dot_f32(v_ref[0, :, low : off + CONT], p.astype(bf16)))


def head_spec(row):
    return pl.BlockSpec((1, HD, GLEN), lambda i: (row, 0, 0))


def whole(*shape):
    return pl.BlockSpec(shape, lambda i: (0,) * len(shape))


def attn_fwd(head, qkv, doc_start, key_bias):
    heads = qkv.shape[0] // 3
    return pl.pallas_call(
        fwd_kernel,
        grid=(1,),
        in_specs=[
            head_spec(head),
            head_spec(head + heads),
            head_spec(head + 2 * heads),
            whole(1, PROMPT),
            whole(GLEN - PROMPT, 128),
        ],
        out_specs=[whole(1, HD, GLEN), whole(1, HD, GLEN), whole(1, 1, GLEN)],
        out_shape=[
            jax.ShapeDtypeStruct((1, HD, GLEN), bf16),
            jax.ShapeDtypeStruct((1, HD, GLEN), f32),
            jax.ShapeDtypeStruct((1, 1, GLEN), f32),
        ],
        scratch_shapes=[pltpu.VMEM((GLEN, HD), bf16)],
        cost_estimate=pl.CostEstimate(flops=17_000_000_000, transcendentals=0, bytes_accessed=4_000_000),
        name="attn_fwd",
    )(qkv, qkv, qkv, doc_start, key_bias)


KEYS = 512
SPAN = 512


def bwd_kernel(
    q_ref, k_ref, v_ref, g_ref, wide_ref, lse_ref, start_ref, bias_ref,
    out_ref, qn, kn, vn, gn, inner, dq,
):
    qn[...] = q_ref[0].T
    kn[...] = k_ref[0].T
    vn[...] = v_ref[0].T
    gn[...] = g_ref[0].T
    inner[...] = jnp.sum(g_ref[0].astype(f32) * wide_ref[0], 0, keepdims=True)
    dq[...] = jnp.zeros_like(dq)

    def block(key_off, key_span, off, span, mask):
        rows = pl.ds(off, span)
        keys = pl.ds(key_off, key_span)
        s = dot_f32(kn[keys, :], q_ref[0, :, rows])
        if mask is not None:
            s = mask(s)
        p = jnp.exp(s - lse_ref[0, :, rows])
        dp = dot_f32(vn[keys, :], g_ref[0, :, rows])
        ds = (p * (dp - inner[:, rows])).astype(bf16)
        dv = dot_f32(p.astype(bf16), gn[rows, :])
        dk = dot_f32(ds, qn[rows, :])
        dq[:, rows] += dot_f32(k_ref[0, :, keys], ds)
        return dk, dv

    def emit(key_off, key_span, dk, dv):
        out_ref[1, :, pl.ds(key_off, key_span)] = dk.T.astype(bf16)
        out_ref[2, :, pl.ds(key_off, key_span)] = dv.T.astype(bf16)

    def key_block(b, carry):
        key_off = pl.multiple_of(b * KEYS, KEYS)

        def continuation(c, acc):
            off = pl.multiple_of(PROMPT + c * SPAN, SPAN)
            dk, dv = block(key_off, KEYS, off, SPAN, None)
            return acc[0] + dk, acc[1] + dv

        zero = jnp.zeros((KEYS, HD), f32)
        acc = lax.fori_loop(0, (GLEN - PROMPT) // SPAN, continuation, (zero, zero))

        def prompt(i, acc):
            off = pl.multiple_of(i * CONT, CONT)

            def mask(s):
                key_ids = key_off + lax.broadcasted_iota(jnp.int32, s.shape, 0)
                row_ids = off + lax.broadcasted_iota(jnp.int32, s.shape, 1)
                keep = (key_ids <= row_ids) & (key_ids >= start_ref[:, pl.ds(off, CONT)])
                return jnp.where(keep, s, NEG)

            dk, dv = block(key_off, KEYS, off, CONT, mask)
            return acc[0] + dk, acc[1] + dv

        last = jnp.minimum((key_off + KEYS + DOC_MAX - 2) // CONT + 1, PROMPT // CONT)
        acc = lax.fori_loop(key_off // CONT, last, prompt, acc)
        emit(key_off, KEYS, *acc)
        return carry

    lax.fori_loop(0, PROMPT // KEYS, key_block, 0)
    causal = lax.broadcasted_iota(jnp.int32, (CONT, CONT), 0) <= lax.broadcasted_iota(
        jnp.int32, (CONT, CONT), 1
    )

    def own(c, carry):
        off = pl.multiple_of(PROMPT + c * CONT, CONT)
        bias = bias_ref[pl.ds(pl.multiple_of(c * CONT, CONT), CONT), :]

        def mask(s):
            return jnp.where(causal, s + jnp.concatenate([bias, bias], 1), NEG)

        emit(off, CONT, *block(off, CONT, off, CONT, mask))
        return carry

    lax.fori_loop(0, CONTS, own, 0)
    out_ref[0] = (dq[...] * SCALE).astype(bf16)


def attn_bwd(head, grads, qkv, adj, wide, lse, doc_start, key_bias):
    heads = qkv.shape[0] // 3
    specs = [
        head_spec(head),
        head_spec(head + heads),
        head_spec(head + 2 * heads),
        whole(1, HD, GLEN),
        whole(1, HD, GLEN),
        whole(1, 1, GLEN),
        whole(1, PROMPT),
        whole(GLEN - PROMPT, 128),
    ]
    args = [qkv, qkv, qkv, adj, wide, lse, doc_start, key_bias]
    kernel = bwd_kernel
    aliases = {}
    if grads is not None:
        specs.append(pl.BlockSpec(memory_space=pl.ANY))
        aliases = {len(args): 0}
        args.append(grads)
        kernel = lambda *refs: bwd_kernel(*refs[:8], *refs[9:])
    return pl.pallas_call(
        kernel,
        grid=(1,),
        in_specs=specs,
        out_specs=pl.BlockSpec((3, None, HD, GLEN), lambda i: (0, head, 0, 0)),
        out_shape=jax.ShapeDtypeStruct((3, heads, HD, GLEN), bf16),
        scratch_shapes=[pltpu.VMEM((GLEN, HD), bf16)] * 4
        + [pltpu.VMEM((1, GLEN), f32), pltpu.VMEM((HD, GLEN), f32)],
        input_output_aliases=aliases,
        cost_estimate=pl.CostEstimate(flops=30_000_000_000, transcendentals=0, bytes_accessed=8_000_000),
        name="attn_bwd",
    )(*args)


def normalize(values):
    centred = values - jnp.mean(values, axis=-1, keepdims=True)
    spread = jnp.mean(centred * centred, axis=-1, keepdims=True)
    return centred * lax.rsqrt(spread + norm_eps)


def affine_norm(values, norm_gain, norm_shift):
    return normalize(values) * norm_gain + norm_shift


def tanh_gelu(values):
    return jax.nn.gelu(values, approximate=True)


def dot(a, b, ca, cb):
    return lax.dot_general(a, b, (((ca,), (cb,)), ((), ())), preferred_element_type=f32)


def swap(x, bit, axis="tensor"):
    size = lax.axis_size(axis)
    return lax.ppermute(x, axis, [(i, i ^ bit) for i in range(size)])


def butterfly(x, axis):
    bit = 1
    while bit < lax.axis_size(axis):
        x = x + swap(x, bit, axis)
        bit *= 2
    return x


def levels(axis):
    steps, shift, size = [], 0, lax.axis_size(axis)
    while 1 << shift < size:
        members = 2 if shift == 0 or size >> shift < 4 else 4
        steps.append((shift, members))
        shift += members.bit_length() - 1
    return steps


def sum_scatter(x, axis):
    for shift, members in levels(axis):
        digit = (lax.axis_index(axis) >> shift) & (members - 1)
        x = x.reshape(members, x.shape[0] // members, x.shape[1])
        total = lax.dynamic_index_in_dim(x, digit, 0, False)
        for j in range(1, members):
            sent = lax.dynamic_index_in_dim(x, digit ^ j, 0, False).astype(bf16)
            total = total + swap(sent, j << shift, axis).astype(f32)
        x = total
    return x.astype(bf16)


def spread(x, axis):
    for shift, members in reversed(levels(axis)):
        digit = (lax.axis_index(axis) >> shift) & (members - 1)
        parts = [x] + [swap(x, j << shift, axis) for j in range(1, members)]
        rows = []
        for i in range(members):
            row = parts[0]
            for j in range(1, members):
                row = jnp.where(digit ^ j == i, parts[j], row)
            rows.append(row)
        x = jnp.concatenate(rows, 0)
    return x.astype(f32)


def sum_all(x, axis):
    return spread(sum_scatter(x, axis), axis)


def gather4(x):
    far = swap(x, 2)
    near = swap(x, 1)
    return [x, near, far, swap(far, 1)]


def scatter4(parts):
    near3 = swap(parts[3], 1)
    near1 = swap(parts[1], 1)
    across = (parts[2].astype(f32) + near3.astype(f32)).astype(bf16)
    mine = parts[0].astype(f32) + near1.astype(f32)
    return mine + swap(across, 2).astype(f32)


def layer(
    layer_input,
    out_cotangent,
    teacher,
    valid_mask,
    prompt_docs,
    pass_embed,
    first_gain,
    first_shift,
    project_in,
    project_out,
    second_gain,
    second_shift,
    expand_weight,
    reduce_weight,
):
    rows = layer_input.shape[0]
    width = project_out.shape[0]
    heads = width // HD
    t = lax.axis_index("tensor")
    slots = [t ^ k for k in range(4)]
    valid = valid_mask[0]
    docs = prompt_docs[0]
    valid_total = butterfly(jnp.sum(valid).astype(f32).reshape(1, 1), "dp")[0, 0]
    divisor = valid_total * D
    doc_start = jnp.zeros_like(docs)
    for v in range(3):
        doc_start = doc_start + jnp.where(docs > v, jnp.sum((docs == v).astype(jnp.int32)), 0)
    doc_start = doc_start[None, :]
    key_bias = jnp.broadcast_to(jnp.where(valid == 1, 0.0, NEG).astype(f32)[:, None], (GLEN - PROMPT, 128))
    row_valid = lax.dynamic_slice_in_dim(
        jnp.concatenate([jnp.zeros((PROMPT,), f32), valid.astype(f32)]), t * rows, rows
    )[:, None]

    hidden_in = layer_input.astype(f32) + pass_embed
    first_affine, first_pull = jax.vjp(affine_norm, hidden_in, first_gain, first_shift)
    first_blocks = gather4(first_affine.astype(bf16))
    in_matrix = project_in.reshape(D, 3 * width)

    expand_weight, reduce_weight, project_out, _ = lax.optimization_barrier(
        (expand_weight, reduce_weight, project_out, first_blocks[2])
    )
    out_blocks = gather4(project_out)
    expand_blocks = gather4(expand_weight)
    reduce_blocks = gather4(reduce_weight)
    out_full = jnp.concatenate(out_blocks, 0)

    qkv = jnp.zeros((3 * width, GLEN), bf16)
    for k in range(4):
        part = dot(in_matrix, first_blocks[k], 0, 1).astype(bf16)
        part = jnp.concatenate([part[:width] * SCALE, part[width:]], 0)
        qkv = lax.dynamic_update_slice(qkv, part, (0, slots[k] * rows))
    qkv = qkv.reshape(3 * heads, HD, GLEN)
    saved = []
    for h in range(heads):
        saved.append(attn_fwd(h, qkv, doc_start, key_bias))
    groups = [saved[:-1], saved[-1:]]
    moved = []
    for group in groups:
        att = jnp.concatenate([x[0][0] for x in group], 0)
        cut = lambda k: lax.dynamic_slice(att, (0, slots[k] * rows), (att.shape[0], rows))
        got = {k: swap(cut(k), k) for k in (3, 2, 1)}
        got[0] = cut(0)
        moved.append(got)
    att_own = jnp.concatenate([got[k] for k in range(4) for got in moved], 0)
    attn_branch = dot(att_own, out_full, 0, 0)
    middle = hidden_in + attn_branch
    second_affine, second_pull = jax.vjp(affine_norm, middle, second_gain, second_shift)
    second_norm = second_affine.astype(bf16)
    acts, pulls = [], []
    mlp_branch = 0.0
    for k in range(4):
        pre_act = dot(second_norm, expand_blocks[k], 1, 0)
        activated, pull = jax.vjp(tanh_gelu, pre_act)
        acts.append(activated.astype(bf16))
        pulls.append(pull)
        mlp_branch = mlp_branch + dot(acts[k], reduce_blocks[k], 1, 0)
    layer_out = middle + mlp_branch
    deviation = row_valid * (layer_out - teacher.astype(f32))
    squares_part = jnp.sum(deviation * deviation)
    out_adj = out_cotangent.astype(f32) + 2.0 / divisor * deviation
    branch_adj = out_adj.astype(bf16)
    second_adj = 0.0
    reduce_parts = [dot(acts[k], branch_adj, 0, 0).astype(bf16) for k in range(4)]
    branch_adj, *reduce_parts = lax.optimization_barrier((branch_adj, *reduce_parts))
    reduce_grad = sum_all(scatter4(reduce_parts), "dp")
    pre_adjs = []
    for k in range(4):
        act_adj = dot(branch_adj, reduce_blocks[k], 1, 1)
        pre_adjs.append(pulls[k](act_adj)[0].astype(bf16))
        second_adj = second_adj + dot(pre_adjs[k], expand_blocks[k], 1, 1)
    middle_part, second_gain_part, second_shift_part = second_pull(second_adj)
    middle_adj = out_adj + middle_part
    attn_adj = middle_adj.astype(bf16)
    att_adj = dot(out_full, attn_adj, 1, 1).astype(bf16)
    att_adj = att_adj.reshape(4, heads, HD, rows)
    adj_heads = []
    for first, last in ((0, 1), (1, heads)):
        full = jnp.zeros(((last - first) * HD, GLEN), bf16)
        for k in (3, 2, 1, 0):
            piece = att_adj[k, first:last].reshape((last - first) * HD, rows)
            piece = swap(piece, k) if k else piece
            full = lax.dynamic_update_slice(full, piece, (0, slots[k] * rows))
        adj_heads += [full[h * HD : (h + 1) * HD][None] for h in range(last - first)]

    expand_parts = [dot(second_norm, pre_adjs[k], 0, 0).astype(bf16) for k in range(4)]
    out_parts = dot(att_own, attn_adj, 1, 0).astype(bf16)
    other_parts = [
        jnp.concatenate([expand_parts[k], out_parts[k * width : (k + 1) * width]], 0) for k in range(4)
    ]
    adj_heads[0], *other_parts = lax.optimization_barrier((adj_heads[0], *other_parts))
    other_grad = sum_all(scatter4(other_parts), "dp")

    proj_adj = None
    for h in range(heads):
        proj_adj = attn_bwd(h, proj_adj, qkv, adj_heads[h], *saved[h][1:], doc_start, key_bias)
    proj_adj = proj_adj.reshape(3 * width, GLEN)
    pieces = [lax.dynamic_slice(proj_adj, (0, slots[k] * rows), (3 * width, rows)) for k in range(4)]
    first_parts = [dot(pieces[k], in_matrix, 0, 1).astype(bf16) for k in range(4)]
    first_adj = scatter4(first_parts)
    in_proj_grad = 0.0
    for k in range(4):
        in_proj_grad = in_proj_grad + dot(first_blocks[k], pieces[k], 0, 1)
    in_proj_grad = sum_all(in_proj_grad, "dp")
    hidden_part, first_gain_part, first_shift_part = first_pull(first_adj)
    input_adj = middle_adj + hidden_part
    embed_part = jnp.sum(input_adj, axis=0)
    small = jnp.stack(
        [
            embed_part,
            first_gain_part,
            first_shift_part,
            second_gain_part,
            second_shift_part,
            jnp.full((D,), squares_part),
        ]
    )
    small = butterfly(butterfly(small, "tensor"), "dp")
    return (
        layer_out.astype(bf16),
        small[5, 0] / divisor,
        input_adj.astype(bf16),
        small[0],
        small[1],
        small[2],
        in_proj_grad.reshape(D, 3, width),
        other_grad[D:],
        small[3],
        small[4],
        other_grad[:D],
        reduce_grad,
    )


def solution(mesh):
    rows = P(("dp", "tensor"), None)
    return jax.shard_map(
        layer,
        mesh=mesh,
        in_specs=(
            rows,
            rows,
            rows,
            P("dp", None),
            P("dp", None),
            P(),
            P(),
            P(),
            P(None, None, "tensor"),
            P("tensor", None),
            P(),
            P(),
            P(None, "tensor"),
            P("tensor", None),
        ),
        out_specs=(
            rows,
            P(),
            rows,
            P(),
            P(),
            P(),
            P(None, None, "tensor"),
            P("tensor", None),
            P(),
            P(),
            P(None, "tensor"),
            P("tensor", None),
        ),
        check_vma=False,
    )
```

```python
import jax
import jax.numpy as jnp
from jax import lax
from jax.experimental import pallas as pl
from jax.experimental.pallas import tpu as pltpu
from jax.sharding import PartitionSpec as P


D = 768
H = 12
HD = D // H
PROMPT = 2048
CONT = 256
CONTS = 8
GLEN = 4096
DOC_MAX = 1024
NEG = -1e30
SCALE = HD ** (-0.5)
norm_eps = 1e-05
bf16 = jnp.bfloat16
f32 = jnp.float32


def dot_f32(a, b):
    return jnp.dot(a, b, preferred_element_type=f32)


def fwd_kernel(q_ref, k_ref, v_ref, start_ref, bias_ref, o_ref, wide_ref, lse_ref, keys_ref):
    keys_ref[...] = k_ref[0].T

    def finish(off, top, total, acc):
        out = acc / total
        wide_ref[0, :, pl.ds(off, CONT)] = out
        o_ref[0, :, pl.ds(off, CONT)] = out.astype(bf16)
        lse_ref[0, :, pl.ds(off, CONT)] = top + jnp.log(total)

    causal = lax.broadcasted_iota(jnp.int32, (CONT, CONT), 0) <= lax.broadcasted_iota(
        jnp.int32, (CONT, CONT), 1
    )

    def continuation(c, carry):
        off = pl.multiple_of(PROMPT + c * CONT, CONT)
        queries = q_ref[0, :, pl.ds(off, CONT)]
        s1 = dot_f32(keys_ref[0:PROMPT, :], queries)
        s2 = dot_f32(keys_ref[pl.ds(off, CONT), :], queries)
        bias = bias_ref[pl.ds(pl.multiple_of(c * CONT, CONT), CONT), :]
        s2 = jnp.where(causal, s2 + jnp.concatenate([bias, bias], 1), NEG)
        top = jnp.maximum(jnp.max(s1, 0, keepdims=True), jnp.max(s2, 0, keepdims=True))
        p1 = jnp.exp(s1 - top)
        p2 = jnp.exp(s2 - top)
        total = jnp.sum(p1, 0, keepdims=True) + jnp.sum(p2, 0, keepdims=True)
        acc = dot_f32(v_ref[0, :, 0:PROMPT], p1.astype(bf16))
        acc = acc + dot_f32(v_ref[0, :, pl.ds(off, CONT)], p2.astype(bf16))
        finish(off, top, total, acc)
        return carry

    lax.fori_loop(0, CONTS, continuation, 0)
    for off in range(0, PROMPT, CONT):
        low = max(0, off - DOC_MAX)
        span = off + CONT - low
        s = dot_f32(keys_ref[low : off + CONT, :], q_ref[0, :, off : off + CONT])
        key_ids = low + lax.broadcasted_iota(jnp.int32, (span, CONT), 0)
        row_ids = off + lax.broadcasted_iota(jnp.int32, (span, CONT), 1)
        s = jnp.where((key_ids <= row_ids) & (key_ids >= start_ref[:, off : off + CONT]), s, NEG)
        top = jnp.max(s, 0, keepdims=True)
        p = jnp.exp(s - top)
        finish(off, top, jnp.sum(p, 0, keepdims=True), dot_f32(v_ref[0, :, low : off + CONT], p.astype(bf16)))


def head_spec(row):
    return pl.BlockSpec((1, HD, GLEN), lambda i: (row, 0, 0))


def whole(*shape):
    return pl.BlockSpec(shape, lambda i: (0,) * len(shape))


def attn_fwd(head, qkv, doc_start, key_bias):
    heads = qkv.shape[0] // 3
    return pl.pallas_call(
        fwd_kernel,
        grid=(1,),
        in_specs=[
            head_spec(head),
            head_spec(head + heads),
            head_spec(head + 2 * heads),
            whole(1, PROMPT),
            whole(GLEN - PROMPT, 128),
        ],
        out_specs=[whole(1, HD, GLEN), whole(1, HD, GLEN), whole(1, 1, GLEN)],
        out_shape=[
            jax.ShapeDtypeStruct((1, HD, GLEN), bf16),
            jax.ShapeDtypeStruct((1, HD, GLEN), f32),
            jax.ShapeDtypeStruct((1, 1, GLEN), f32),
        ],
        scratch_shapes=[pltpu.VMEM((GLEN, HD), bf16)],
        cost_estimate=pl.CostEstimate(flops=17_000_000_000, transcendentals=0, bytes_accessed=4_000_000),
        name="attn_fwd",
    )(qkv, qkv, qkv, doc_start, key_bias)


KEYS = 512
SPAN = 512


def bwd_kernel(
    q_ref, k_ref, v_ref, g_ref, wide_ref, lse_ref, start_ref, bias_ref,
    out_ref, qn, kn, vn, gn, inner, dq,
):
    qn[...] = q_ref[0].T
    kn[...] = k_ref[0].T
    vn[...] = v_ref[0].T
    gn[...] = g_ref[0].T
    inner[...] = jnp.sum(g_ref[0].astype(f32) * wide_ref[0], 0, keepdims=True)
    dq[...] = jnp.zeros_like(dq)

    def block(key_off, key_span, off, span, mask):
        rows = pl.ds(off, span)
        keys = pl.ds(key_off, key_span)
        s = dot_f32(kn[keys, :], q_ref[0, :, rows])
        if mask is not None:
            s = mask(s)
        p = jnp.exp(s - lse_ref[0, :, rows])
        dp = dot_f32(vn[keys, :], g_ref[0, :, rows])
        ds = (p * (dp - inner[:, rows])).astype(bf16)
        dv = dot_f32(p.astype(bf16), gn[rows, :])
        dk = dot_f32(ds, qn[rows, :])
        dq[:, rows] += dot_f32(k_ref[0, :, keys], ds)
        return dk, dv

    def emit(key_off, key_span, dk, dv):
        out_ref[1, :, pl.ds(key_off, key_span)] = dk.T.astype(bf16)
        out_ref[2, :, pl.ds(key_off, key_span)] = dv.T.astype(bf16)

    def key_block(b, carry):
        key_off = pl.multiple_of(b * KEYS, KEYS)

        def continuation(c, acc):
            off = pl.multiple_of(PROMPT + c * SPAN, SPAN)
            dk, dv = block(key_off, KEYS, off, SPAN, None)
            return acc[0] + dk, acc[1] + dv

        zero = jnp.zeros((KEYS, HD), f32)
        acc = lax.fori_loop(0, (GLEN - PROMPT) // SPAN, continuation, (zero, zero))

        def prompt(i, acc):
            off = pl.multiple_of(i * CONT, CONT)

            def mask(s):
                key_ids = key_off + lax.broadcasted_iota(jnp.int32, s.shape, 0)
                row_ids = off + lax.broadcasted_iota(jnp.int32, s.shape, 1)
                keep = (key_ids <= row_ids) & (key_ids >= start_ref[:, pl.ds(off, CONT)])
                return jnp.where(keep, s, NEG)

            dk, dv = block(key_off, KEYS, off, CONT, mask)
            return acc[0] + dk, acc[1] + dv

        last = jnp.minimum((key_off + KEYS + DOC_MAX - 2) // CONT + 1, PROMPT // CONT)
        acc = lax.fori_loop(key_off // CONT, last, prompt, acc)
        emit(key_off, KEYS, *acc)
        return carry

    lax.fori_loop(0, PROMPT // KEYS, key_block, 0)
    causal = lax.broadcasted_iota(jnp.int32, (CONT, CONT), 0) <= lax.broadcasted_iota(
        jnp.int32, (CONT, CONT), 1
    )

    def own(c, carry):
        off = pl.multiple_of(PROMPT + c * CONT, CONT)
        bias = bias_ref[pl.ds(pl.multiple_of(c * CONT, CONT), CONT), :]

        def mask(s):
            return jnp.where(causal, s + jnp.concatenate([bias, bias], 1), NEG)

        emit(off, CONT, *block(off, CONT, off, CONT, mask))
        return carry

    lax.fori_loop(0, CONTS, own, 0)
    out_ref[0] = (dq[...] * SCALE).astype(bf16)


def attn_bwd(head, grads, qkv, adj, wide, lse, doc_start, key_bias):
    heads = qkv.shape[0] // 3
    specs = [
        head_spec(head),
        head_spec(head + heads),
        head_spec(head + 2 * heads),
        whole(1, HD, GLEN),
        whole(1, HD, GLEN),
        whole(1, 1, GLEN),
        whole(1, PROMPT),
        whole(GLEN - PROMPT, 128),
    ]
    args = [qkv, qkv, qkv, adj, wide, lse, doc_start, key_bias]
    kernel = bwd_kernel
    aliases = {}
    if grads is not None:
        specs.append(pl.BlockSpec(memory_space=pl.ANY))
        aliases = {len(args): 0}
        args.append(grads)
        kernel = lambda *refs: bwd_kernel(*refs[:8], *refs[9:])
    return pl.pallas_call(
        kernel,
        grid=(1,),
        in_specs=specs,
        out_specs=pl.BlockSpec((3, None, HD, GLEN), lambda i: (0, head, 0, 0)),
        out_shape=jax.ShapeDtypeStruct((3, heads, HD, GLEN), bf16),
        scratch_shapes=[pltpu.VMEM((GLEN, HD), bf16)] * 4
        + [pltpu.VMEM((1, GLEN), f32), pltpu.VMEM((HD, GLEN), f32)],
        input_output_aliases=aliases,
        cost_estimate=pl.CostEstimate(flops=30_000_000_000, transcendentals=0, bytes_accessed=8_000_000),
        name="attn_bwd",
    )(*args)


def normalize(values):
    centred = values - jnp.mean(values, axis=-1, keepdims=True)
    spread = jnp.mean(centred * centred, axis=-1, keepdims=True)
    return centred * lax.rsqrt(spread + norm_eps)


def affine_norm(values, norm_gain, norm_shift):
    return normalize(values) * norm_gain + norm_shift


GELU_C = 0.7978845608028654
GELU_A = 0.044715
BLOCK = 256


def dot(a, b, ca, cb):
    return lax.dot_general(a, b, (((ca,), (cb,)), ((), ())), preferred_element_type=f32)


def row_norm(values):
    centred = values - jnp.mean(values, axis=-1, keepdims=True)
    rstd = lax.rsqrt(jnp.mean(centred * centred, axis=-1, keepdims=True) + norm_eps)
    return centred * rstd, rstd


def norm_pull(norm, rstd, adj):
    first = jnp.mean(adj, axis=-1, keepdims=True)
    second = jnp.mean(adj * norm, axis=-1, keepdims=True)
    return (adj - first - norm * second) * rstd


def mid_fwd_kernel(
    scale_ref, att_ref, x_ref, embed_ref, gain_ref, shift_ref, teacher_ref, cot_ref, valid_ref,
    out_w, e0, e1, e2, e3, r0, r1, r2, r3,
    layer_ref, norm_ref, act_ref, slope_ref, branch_ref, middle_ref, adj_ref, squares_ref,
):
    hidden = x_ref[...].astype(f32) + embed_ref[...]
    middle = hidden + dot(att_ref[...], out_w[...], 0, 0)
    middle_ref[...] = middle
    normed = (row_norm(middle)[0] * gain_ref[...] + shift_ref[...]).astype(bf16)
    norm_ref[...] = normed
    total = middle
    for k, (expand, reduce) in enumerate(((e0, r0), (e1, r1), (e2, r2), (e3, r3))):
        u = dot(normed, expand[...], 1, 0)
        square = u * u
        th = jnp.tanh(GELU_C * (u + GELU_A * (u * square)))
        half = 0.5 * (1.0 + th)
        act = (u * half).astype(bf16)
        act_ref[k] = act
        slope_ref[k] = half + (0.5 * GELU_C) * u * (1.0 - th * th) * (1.0 + (3.0 * GELU_A) * square)
        total = total + dot(act, reduce[...], 1, 0)
    layer_ref[...] = total.astype(bf16)
    deviation = valid_ref[...] * (total - teacher_ref[...].astype(f32))
    out_adj = cot_ref[...].astype(f32) + scale_ref[0, 0] * deviation
    adj_ref[...] = out_adj
    branch_ref[...] = out_adj.astype(bf16)

    @pl.when(pl.program_id(0) == 0)
    def _():
        squares_ref[...] = jnp.zeros_like(squares_ref)

    squares_ref[...] += jnp.sum(deviation * deviation, axis=0, keepdims=True)


def mid_bwd_kernel(
    branch_ref, slope_ref, middle_ref, adj_ref, gain_ref, out_w, e0, e1, e2, e3, r0, r1, r2, r3,
    pre_ref, middle_adj_ref, attn_ref, att_ref, gain_out, shift_out,
):
    branch = branch_ref[...]
    second = None
    for k, (expand, reduce) in enumerate(((e0, r0), (e1, r1), (e2, r2), (e3, r3))):
        pre = (dot(branch, reduce[...], 1, 1) * slope_ref[k]).astype(bf16)
        pre_ref[k] = pre
        part = dot(pre, expand[...], 1, 1)
        second = part if second is None else second + part
    norm, rstd = row_norm(middle_ref[...])

    @pl.when(pl.program_id(0) == 0)
    def _():
        gain_out[...] = jnp.zeros_like(gain_out)
        shift_out[...] = jnp.zeros_like(shift_out)

    gain_out[...] += jnp.sum(second * norm, axis=0, keepdims=True)
    shift_out[...] += jnp.sum(second, axis=0, keepdims=True)
    middle_adj = adj_ref[...] + norm_pull(norm, rstd, second * gain_ref[...])
    middle_adj_ref[...] = middle_adj
    attn_adj = middle_adj.astype(bf16)
    attn_ref[...] = attn_adj
    att_ref[...] = dot(out_w[...], attn_adj, 1, 1).astype(bf16)


def fixed(shape):
    return pl.BlockSpec(shape, lambda i: (0,) * len(shape), pipeline_mode=pl.Buffered(1))


def by_rows(width):
    return pl.BlockSpec((BLOCK, width), lambda i: (i, 0))


def by_rows4(width):
    return pl.BlockSpec((4, BLOCK, width), lambda i: (0, i, 0))


def by_cols(height):
    return pl.BlockSpec((height, BLOCK), lambda i: (0, i))


def mid_fwd(scale, att, x, embed, gain, shift, teacher, cot, valid, out_w, expand, reduce):
    rows = x.shape[0]
    width = expand[0].shape[1]
    shape = jax.ShapeDtypeStruct
    return pl.pallas_call(
        mid_fwd_kernel,
        grid=(rows // BLOCK,),
        in_specs=[
            pl.BlockSpec(memory_space=pltpu.SMEM), by_cols(D), by_rows(D), fixed((1, D)), fixed((1, D)),
            fixed((1, D)), by_rows(D), by_rows(D), by_rows(1), fixed((D, D)),
        ] + [fixed((D, width))] * 4 + [fixed((width, D))] * 4,
        out_specs=[
            by_rows(D), by_rows(D), by_rows4(width), by_rows4(width), by_rows(D), by_rows(D), by_rows(D),
            fixed((1, D)),
        ],
        out_shape=[
            shape((rows, D), bf16), shape((rows, D), bf16), shape((4, rows, width), bf16),
            shape((4, rows, width), f32), shape((rows, D), bf16), shape((rows, D), f32),
            shape((rows, D), f32), shape((1, D), f32),
        ],
        cost_estimate=pl.CostEstimate(flops=22_000_000_000, transcendentals=0, bytes_accessed=30_000_000),
        name="mid_fwd",
    )(scale, att, x, embed, gain, shift, teacher, cot, valid, out_w, *expand, *reduce)


def mid_bwd(branch, slope, middle, adj, gain, out_w, expand, reduce):
    rows = branch.shape[0]
    width = expand[0].shape[1]
    shape = jax.ShapeDtypeStruct
    return pl.pallas_call(
        mid_bwd_kernel,
        grid=(rows // BLOCK,),
        in_specs=[by_rows(D), by_rows4(width), by_rows(D), by_rows(D), fixed((1, D)), fixed((D, D))]
        + [fixed((D, width))] * 4 + [fixed((width, D))] * 4,
        out_specs=[by_rows4(width), by_rows(D), by_rows(D), by_cols(D), fixed((1, D)), fixed((1, D))],
        out_shape=[
            shape((4, rows, width), bf16), shape((rows, D), f32), shape((rows, D), bf16),
            shape((D, rows), bf16), shape((1, D), f32), shape((1, D), f32),
        ],
        cost_estimate=pl.CostEstimate(flops=22_000_000_000, transcendentals=0, bytes_accessed=30_000_000),
        name="mid_bwd",
    )(branch, slope, middle, adj, gain, out_w, *expand, *reduce)


def swap(x, bit, axis="tensor"):
    size = lax.axis_size(axis)
    return lax.ppermute(x, axis, [(i, i ^ bit) for i in range(size)])


def butterfly(x, axis):
    bit = 1
    while bit < lax.axis_size(axis):
        x = x + swap(x, bit, axis)
        bit *= 2
    return x


def levels(axis):
    steps, shift, size = [], 0, lax.axis_size(axis)
    while 1 << shift < size:
        members = 2 if shift == 0 or size >> shift < 4 else 4
        steps.append((shift, members))
        shift += members.bit_length() - 1
    return steps


def sum_scatter(x, axis):
    for shift, members in levels(axis):
        digit = (lax.axis_index(axis) >> shift) & (members - 1)
        x = x.reshape(members, x.shape[0] // members, x.shape[1])
        total = lax.dynamic_index_in_dim(x, digit, 0, False)
        for j in range(1, members):
            sent = lax.dynamic_index_in_dim(x, digit ^ j, 0, False).astype(bf16)
            total = total + swap(sent, j << shift, axis).astype(f32)
        x = total
    return x.astype(bf16)


def spread(x, axis):
    for shift, members in reversed(levels(axis)):
        digit = (lax.axis_index(axis) >> shift) & (members - 1)
        parts = [x] + [swap(x, j << shift, axis) for j in range(1, members)]
        rows = []
        for i in range(members):
            row = parts[0]
            for j in range(1, members):
                row = jnp.where(digit ^ j == i, parts[j], row)
            rows.append(row)
        x = jnp.concatenate(rows, 0)
    return x.astype(f32)


def sum_all(x, axis):
    return spread(sum_scatter(x, axis), axis)


def gather4(x):
    far = swap(x, 2)
    near = swap(x, 1)
    return [x, near, far, swap(far, 1)]


def scatter4(parts):
    near3 = swap(parts[3], 1)
    near1 = swap(parts[1], 1)
    across = (parts[2].astype(f32) + near3.astype(f32)).astype(bf16)
    mine = parts[0].astype(f32) + near1.astype(f32)
    return mine + swap(across, 2).astype(f32)


def layer(
    layer_input,
    out_cotangent,
    teacher,
    valid_mask,
    prompt_docs,
    pass_embed,
    first_gain,
    first_shift,
    project_in,
    project_out,
    second_gain,
    second_shift,
    expand_weight,
    reduce_weight,
):
    rows = layer_input.shape[0]
    width = project_out.shape[0]
    heads = width // HD
    t = lax.axis_index("tensor")
    slots = [t ^ k for k in range(4)]
    valid = valid_mask[0]
    docs = prompt_docs[0]
    valid_total = butterfly(jnp.sum(valid).astype(f32).reshape(1, 1), "dp")[0, 0]
    divisor = valid_total * D
    doc_start = jnp.zeros_like(docs)
    for v in range(3):
        doc_start = doc_start + jnp.where(docs > v, jnp.sum((docs == v).astype(jnp.int32)), 0)
    doc_start = doc_start[None, :]
    key_bias = jnp.broadcast_to(jnp.where(valid == 1, 0.0, NEG).astype(f32)[:, None], (GLEN - PROMPT, 128))
    row_valid = lax.dynamic_slice_in_dim(
        jnp.concatenate([jnp.zeros((PROMPT,), f32), valid.astype(f32)]), t * rows, rows
    )[:, None]

    hidden_in = layer_input.astype(f32) + pass_embed
    first_affine, first_pull = jax.vjp(affine_norm, hidden_in, first_gain, first_shift)
    first_blocks = gather4(first_affine.astype(bf16))
    in_matrix = project_in.reshape(D, 3 * width)

    expand_weight, reduce_weight, project_out, _ = lax.optimization_barrier(
        (expand_weight, reduce_weight, project_out, first_blocks[2])
    )
    out_blocks = gather4(project_out)
    expand_blocks = gather4(expand_weight)
    reduce_blocks = gather4(reduce_weight)
    out_full = jnp.concatenate(out_blocks, 0)

    qkv = jnp.zeros((3 * width, GLEN), bf16)
    for k in range(4):
        part = dot(in_matrix, first_blocks[k], 0, 1).astype(bf16)
        part = jnp.concatenate([part[:width] * SCALE, part[width:]], 0)
        qkv = lax.dynamic_update_slice(qkv, part, (0, slots[k] * rows))
    qkv = qkv.reshape(3 * heads, HD, GLEN)
    saved = []
    for h in range(heads):
        saved.append(attn_fwd(h, qkv, doc_start, key_bias))
    groups = [saved[:-1], saved[-1:]]
    moved = []
    for group in groups:
        att = jnp.concatenate([x[0][0] for x in group], 0)
        cut = lambda k: lax.dynamic_slice(att, (0, slots[k] * rows), (att.shape[0], rows))
        got = {k: swap(cut(k), k) for k in (3, 2, 1)}
        got[0] = cut(0)
        moved.append(got)
    att_own = jnp.concatenate([got[k] for k in range(4) for got in moved], 0)
    layer_out, second_norm, acts, slope, branch_adj, middle, out_adj, squares = mid_fwd(
        (2.0 / divisor).reshape(1, 1), att_own, layer_input, pass_embed[None], second_gain[None],
        second_shift[None], teacher, out_cotangent, row_valid, out_full, expand_blocks, reduce_blocks,
    )
    reduce_parts = [dot(acts[k], branch_adj, 0, 0).astype(bf16) for k in range(4)]
    branch_adj, *reduce_parts = lax.optimization_barrier((branch_adj, *reduce_parts))
    reduce_grad = sum_all(scatter4(reduce_parts), "dp")
    pre_adjs, middle_adj, attn_adj, att_adj, second_gain_part, second_shift_part = mid_bwd(
        branch_adj, slope, middle, out_adj, second_gain[None], out_full, expand_blocks, reduce_blocks
    )
    att_adj = att_adj.reshape(4, heads, HD, rows)
    adj_heads = []
    for first, last in ((0, 1), (1, heads)):
        full = jnp.zeros(((last - first) * HD, GLEN), bf16)
        for k in (3, 2, 1, 0):
            piece = att_adj[k, first:last].reshape((last - first) * HD, rows)
            piece = swap(piece, k) if k else piece
            full = lax.dynamic_update_slice(full, piece, (0, slots[k] * rows))
        adj_heads += [full[h * HD : (h + 1) * HD][None] for h in range(last - first)]

    expand_parts = [dot(second_norm, pre_adjs[k], 0, 0).astype(bf16) for k in range(4)]
    out_parts = dot(att_own, attn_adj, 1, 0).astype(bf16)
    other_parts = [
        jnp.concatenate([expand_parts[k], out_parts[k * width : (k + 1) * width]], 0) for k in range(4)
    ]
    adj_heads[0], *other_parts = lax.optimization_barrier((adj_heads[0], *other_parts))
    other_grad = sum_all(scatter4(other_parts), "dp")

    proj_adj = None
    for h in range(heads):
        proj_adj = attn_bwd(h, proj_adj, qkv, adj_heads[h], *saved[h][1:], doc_start, key_bias)
    proj_adj = proj_adj.reshape(3 * width, GLEN)
    pieces = [lax.dynamic_slice(proj_adj, (0, slots[k] * rows), (3 * width, rows)) for k in range(4)]
    first_parts = [dot(pieces[k], in_matrix, 0, 1).astype(bf16) for k in range(4)]
    first_adj = scatter4(first_parts)
    in_proj_grad = 0.0
    for k in range(4):
        in_proj_grad = in_proj_grad + dot(first_blocks[k], pieces[k], 0, 1)
    in_proj_grad = sum_all(in_proj_grad, "dp")
    hidden_part, first_gain_part, first_shift_part = first_pull(first_adj)
    input_adj = middle_adj + hidden_part
    embed_part = jnp.sum(input_adj, axis=0)
    small = jnp.stack(
        [
            embed_part,
            first_gain_part,
            first_shift_part,
            second_gain_part[0],
            second_shift_part[0],
            squares[0],
        ]
    )
    small = butterfly(butterfly(small, "tensor"), "dp")
    return (
        layer_out,
        jnp.sum(small[5]) / divisor,
        input_adj.astype(bf16),
        small[0],
        small[1],
        small[2],
        in_proj_grad.reshape(D, 3, width),
        other_grad[D:],
        small[3],
        small[4],
        other_grad[:D],
        reduce_grad,
    )


def solution(mesh):
    rows = P(("dp", "tensor"), None)
    return jax.shard_map(
        layer,
        mesh=mesh,
        in_specs=(
            rows,
            rows,
            rows,
            P("dp", None),
            P("dp", None),
            P(),
            P(),
            P(),
            P(None, None, "tensor"),
            P("tensor", None),
            P(),
            P(),
            P(None, "tensor"),
            P("tensor", None),
        ),
        out_specs=(
            rows,
            P(),
            rows,
            P(),
            P(),
            P(),
            P(None, None, "tensor"),
            P("tensor", None),
            P(),
            P(),
            P(None, "tensor"),
            P("tensor", None),
        ),
        check_vma=False,
    )
```

```python
import jax
import jax.numpy as jnp
from jax import lax
from jax.experimental import pallas as pl
from jax.experimental.pallas import tpu as pltpu
from jax.sharding import PartitionSpec as P


D = 768
H = 12
HD = D // H
PROMPT = 2048
CONT = 256
CONTS = 8
GLEN = 4096
DOC_MAX = 1024
NEG = -1e30
SCALE = HD ** (-0.5)
norm_eps = 1e-05
bf16 = jnp.bfloat16
f32 = jnp.float32


def dot_f32(a, b):
    return jnp.dot(a, b, preferred_element_type=f32)


def split3(x):
    high = x.astype(bf16)
    rest = x - high.astype(f32)
    middle = rest.astype(bf16)
    return high, middle, (rest - middle.astype(f32)).astype(bf16)


def fwd_kernel(q_ref, k_ref, v_ref, start_ref, bias_ref, o_ref, wide_ref, lse_ref, keys_ref):
    keys_ref[...] = k_ref[0].T

    def finish(off, top, total, acc):
        out = acc / total
        wide_ref[0, :, pl.ds(off, CONT)] = out
        o_ref[0, :, pl.ds(off, CONT)] = out.astype(bf16)
        lse_ref[0, :, pl.ds(off, CONT)] = top + jnp.log(total)

    causal = lax.broadcasted_iota(jnp.int32, (CONT, CONT), 0) <= lax.broadcasted_iota(
        jnp.int32, (CONT, CONT), 1
    )

    def continuation(c, carry):
        off = pl.multiple_of(PROMPT + c * CONT, CONT)
        queries = q_ref[0, :, pl.ds(off, CONT)]
        s1 = dot_f32(keys_ref[0:PROMPT, :], queries)
        s2 = dot_f32(keys_ref[pl.ds(off, CONT), :], queries)
        bias = bias_ref[pl.ds(pl.multiple_of(c * CONT, CONT), CONT), :]
        s2 = jnp.where(causal, s2 + jnp.concatenate([bias, bias], 1), NEG)
        top = jnp.maximum(jnp.max(s1, 0, keepdims=True), jnp.max(s2, 0, keepdims=True))
        p1 = jnp.exp(s1 - top)
        p2 = jnp.exp(s2 - top)
        total = jnp.sum(p1, 0, keepdims=True) + jnp.sum(p2, 0, keepdims=True)
        acc = dot_f32(v_ref[0, :, 0:PROMPT], p1.astype(bf16))
        acc = acc + dot_f32(v_ref[0, :, pl.ds(off, CONT)], p2.astype(bf16))
        finish(off, top, total, acc)
        return carry

    lax.fori_loop(0, CONTS, continuation, 0)
    for off in range(0, PROMPT, CONT):
        low = max(0, off - DOC_MAX)
        span = off + CONT - low
        s = dot_f32(keys_ref[low : off + CONT, :], q_ref[0, :, off : off + CONT])
        key_ids = low + lax.broadcasted_iota(jnp.int32, (span, CONT), 0)
        row_ids = off + lax.broadcasted_iota(jnp.int32, (span, CONT), 1)
        s = jnp.where((key_ids <= row_ids) & (key_ids >= start_ref[:, off : off + CONT]), s, NEG)
        top = jnp.max(s, 0, keepdims=True)
        p = jnp.exp(s - top)
        finish(off, top, jnp.sum(p, 0, keepdims=True), dot_f32(v_ref[0, :, low : off + CONT], p.astype(bf16)))


def head_spec(row):
    return pl.BlockSpec((1, HD, GLEN), lambda i: (row, 0, 0))


def whole(*shape):
    return pl.BlockSpec(shape, lambda i: (0,) * len(shape))


def attn_fwd(head, qkv, doc_start, key_bias):
    heads = qkv.shape[0] // 3
    return pl.pallas_call(
        fwd_kernel,
        grid=(1,),
        in_specs=[
            head_spec(head),
            head_spec(head + heads),
            head_spec(head + 2 * heads),
            whole(1, PROMPT),
            whole(GLEN - PROMPT, 128),
        ],
        out_specs=[whole(1, HD, GLEN), whole(1, HD, GLEN), whole(1, 1, GLEN)],
        out_shape=[
            jax.ShapeDtypeStruct((1, HD, GLEN), bf16),
            jax.ShapeDtypeStruct((1, HD, GLEN), f32),
            jax.ShapeDtypeStruct((1, 1, GLEN), f32),
        ],
        scratch_shapes=[pltpu.VMEM((GLEN, HD), bf16)],
        cost_estimate=pl.CostEstimate(flops=17_000_000_000, transcendentals=0, bytes_accessed=4_000_000),
        name="attn_fwd",
    )(qkv, qkv, qkv, doc_start, key_bias)


SMEM_SPEC = pl.BlockSpec(memory_space=pltpu.SMEM)
KEYS = 512
SPAN = 1024


def bwd_kernel(
    last_ref, q_ref, k_ref, v_ref, g_ref, wide_ref, lse_ref, start_ref, bias_ref,
    out_ref, qn, kn, vn, gn, qx, gx, dq,
):
    qn[...] = q_ref[0].T
    gn[...] = g_ref[0].T
    ones = jnp.where(lax.broadcasted_iota(jnp.int32, (GLEN, HD), 1) < 3, 1.0, 0.0).astype(bf16)
    kn[:, :HD] = k_ref[0].T
    kn[:, HD:] = ones
    vn[:, :HD] = v_ref[0].T
    vn[:, HD:] = ones
    zeros = jnp.zeros((HD - 16, GLEN), bf16)
    row = lax.broadcasted_iota(jnp.int32, (16, GLEN), 0)

    def extend(ref, head, tail):
        ref[0:HD, :] = head
        a, b, c = (jnp.broadcast_to(x.astype(f32), (16, GLEN)) for x in split3(-tail))
        ref[HD : HD + 16, :] = jnp.where(
            row == 0, a, jnp.where(row == 1, b, jnp.where(row == 2, c, 0.0))
        ).astype(bf16)
        ref[HD + 16 :, :] = zeros

    extend(qx, q_ref[0], lse_ref[0])
    extend(gx, g_ref[0], jnp.sum(g_ref[0].astype(f32) * wide_ref[0], 0, keepdims=True))
    dq[...] = jnp.zeros_like(dq)

    def block(key_off, key_span, off, span, mask):
        rows = pl.ds(off, span)
        keys = pl.ds(key_off, key_span)
        s = dot_f32(kn[keys, :], qx[:, rows])
        if mask is not None:
            s = mask(s)
        p = jnp.exp(s)
        ds = (p * dot_f32(vn[keys, :], gx[:, rows])).astype(bf16)
        dv = dot_f32(p.astype(bf16), gn[rows, :])
        dk = dot_f32(ds, qn[rows, :])
        dq[:, rows] += dot_f32(k_ref[0, :, keys], ds)
        return dk, dv

    def emit(key_off, key_span, dk, dv):
        out_ref[1, :, pl.ds(key_off, key_span)] = dk.T.astype(bf16)
        out_ref[2, :, pl.ds(key_off, key_span)] = dv.T.astype(bf16)

    def key_block(b, carry):
        key_off = pl.multiple_of(b * KEYS, KEYS)

        def continuation(c, acc):
            off = pl.multiple_of(PROMPT + c * SPAN, SPAN)
            dk, dv = block(key_off, KEYS, off, SPAN, None)
            return acc[0] + dk, acc[1] + dv

        zero = jnp.zeros((KEYS, HD), f32)
        acc = lax.fori_loop(0, (GLEN - PROMPT) // SPAN, continuation, (zero, zero))

        def prompt(i, acc):
            off = pl.multiple_of(i * CONT, CONT)

            def mask(s):
                key_ids = key_off + lax.broadcasted_iota(jnp.int32, s.shape, 0)
                row_ids = off + lax.broadcasted_iota(jnp.int32, s.shape, 1)
                keep = (key_ids <= row_ids) & (key_ids >= start_ref[:, pl.ds(off, CONT)])
                return jnp.where(keep, s, NEG)

            dk, dv = block(key_off, KEYS, off, CONT, mask)
            return acc[0] + dk, acc[1] + dv

        first = key_off // CONT
        acc = lax.fori_loop(first, last_ref[first + KEYS // CONT - 1], prompt, acc)
        emit(key_off, KEYS, *acc)
        return carry

    lax.fori_loop(0, PROMPT // KEYS, key_block, 0)
    causal = lax.broadcasted_iota(jnp.int32, (CONT, CONT), 0) <= lax.broadcasted_iota(
        jnp.int32, (CONT, CONT), 1
    )

    def own(c, carry):
        off = pl.multiple_of(PROMPT + c * CONT, CONT)
        bias = bias_ref[pl.ds(pl.multiple_of(c * CONT, CONT), CONT), :]

        def mask(s):
            return jnp.where(causal, s + jnp.concatenate([bias, bias], 1), NEG)

        emit(off, CONT, *block(off, CONT, off, CONT, mask))
        return carry

    lax.fori_loop(0, CONTS, own, 0)
    out_ref[0] = (dq[...] * SCALE).astype(bf16)


def attn_bwd(head, grads, bounds, qkv, adj, wide, lse, doc_start, key_bias):
    heads = qkv.shape[0] // 3
    specs = [
        SMEM_SPEC,
        head_spec(head),
        head_spec(head + heads),
        head_spec(head + 2 * heads),
        whole(1, HD, GLEN),
        whole(1, HD, GLEN),
        whole(1, 1, GLEN),
        whole(1, PROMPT),
        whole(GLEN - PROMPT, 128),
    ]
    args = [bounds, qkv, qkv, qkv, adj, wide, lse, doc_start, key_bias]
    kernel = bwd_kernel
    aliases = {}
    if grads is not None:
        specs.append(pl.BlockSpec(memory_space=pl.ANY))
        aliases = {len(args): 0}
        args.append(grads)
        kernel = lambda *refs: bwd_kernel(*refs[:9], *refs[10:])
    return pl.pallas_call(
        kernel,
        grid=(1,),
        in_specs=specs,
        out_specs=pl.BlockSpec((3, None, HD, GLEN), lambda i: (0, head, 0, 0)),
        out_shape=jax.ShapeDtypeStruct((3, heads, HD, GLEN), bf16),
        scratch_shapes=[
            pltpu.VMEM((GLEN, HD), bf16),
            pltpu.VMEM((GLEN, 2 * HD), bf16),
            pltpu.VMEM((GLEN, 2 * HD), bf16),
            pltpu.VMEM((GLEN, HD), bf16),
            pltpu.VMEM((2 * HD, GLEN), bf16),
            pltpu.VMEM((2 * HD, GLEN), bf16),
            pltpu.VMEM((HD, GLEN), f32),
        ],
        input_output_aliases=aliases,
        cost_estimate=pl.CostEstimate(flops=30_000_000_000, transcendentals=0, bytes_accessed=8_000_000),
        name="attn_bwd",
    )(*args)


def normalize(values):
    centred = values - jnp.mean(values, axis=-1, keepdims=True)
    spread = jnp.mean(centred * centred, axis=-1, keepdims=True)
    return centred * lax.rsqrt(spread + norm_eps)


def affine_norm(values, norm_gain, norm_shift):
    return normalize(values) * norm_gain + norm_shift


GELU_C = 0.7978845608028654
GELU_A = 0.044715
BLOCK = 256


def dot(a, b, ca, cb):
    return lax.dot_general(a, b, (((ca,), (cb,)), ((), ())), preferred_element_type=f32)


def row_norm(values):
    centred = values - jnp.mean(values, axis=-1, keepdims=True)
    rstd = lax.rsqrt(jnp.mean(centred * centred, axis=-1, keepdims=True) + norm_eps)
    return centred * rstd, rstd


def norm_pull(norm, rstd, adj):
    first = jnp.mean(adj, axis=-1, keepdims=True)
    second = jnp.mean(adj * norm, axis=-1, keepdims=True)
    return (adj - first - norm * second) * rstd


def mid_fwd_kernel(
    scale_ref, att_ref, x_ref, embed_ref, gain_ref, shift_ref, teacher_ref, cot_ref, valid_ref,
    out_w, e0, e1, e2, e3, r0, r1, r2, r3,
    layer_ref, norm_ref, act_ref, slope_ref, branch_ref, middle_ref, adj_ref, squares_ref,
):
    hidden = x_ref[...].astype(f32) + embed_ref[...]
    middle = hidden + dot(att_ref[...], out_w[...], 0, 0)
    middle_ref[...] = middle
    normed = (row_norm(middle)[0] * gain_ref[...] + shift_ref[...]).astype(bf16)
    norm_ref[...] = normed
    total = middle
    for k, (expand, reduce) in enumerate(((e0, r0), (e1, r1), (e2, r2), (e3, r3))):
        u = dot(normed, expand[...], 1, 0)
        square = u * u
        th = jnp.tanh(GELU_C * (u + GELU_A * (u * square)))
        half = 0.5 * (1.0 + th)
        act = (u * half).astype(bf16)
        act_ref[k] = act
        slope_ref[k] = half + (0.5 * GELU_C) * u * (1.0 - th * th) * (1.0 + (3.0 * GELU_A) * square)
        total = total + dot(act, reduce[...], 1, 0)
    layer_ref[...] = total.astype(bf16)
    deviation = valid_ref[...] * (total - teacher_ref[...].astype(f32))
    out_adj = cot_ref[...].astype(f32) + scale_ref[0, 0] * deviation
    adj_ref[...] = out_adj
    branch_ref[...] = out_adj.astype(bf16)

    @pl.when(pl.program_id(0) == 0)
    def _():
        squares_ref[...] = jnp.zeros_like(squares_ref)

    squares_ref[...] += jnp.sum(deviation * deviation, axis=0, keepdims=True)


def mid_bwd_kernel(
    branch_ref, slope_ref, middle_ref, adj_ref, gain_ref, out_w, e0, e1, e2, e3, r0, r1, r2, r3,
    pre_ref, middle_adj_ref, attn_ref, att_ref, gain_out, shift_out,
):
    branch = branch_ref[...]
    second = None
    for k, (expand, reduce) in enumerate(((e0, r0), (e1, r1), (e2, r2), (e3, r3))):
        pre = (dot(branch, reduce[...], 1, 1) * slope_ref[k]).astype(bf16)
        pre_ref[k] = pre
        part = dot(pre, expand[...], 1, 1)
        second = part if second is None else second + part
    norm, rstd = row_norm(middle_ref[...])

    @pl.when(pl.program_id(0) == 0)
    def _():
        gain_out[...] = jnp.zeros_like(gain_out)
        shift_out[...] = jnp.zeros_like(shift_out)

    gain_out[...] += jnp.sum(second * norm, axis=0, keepdims=True)
    shift_out[...] += jnp.sum(second, axis=0, keepdims=True)
    middle_adj = adj_ref[...] + norm_pull(norm, rstd, second * gain_ref[...])
    middle_adj_ref[...] = middle_adj
    attn_adj = middle_adj.astype(bf16)
    attn_ref[...] = attn_adj
    att_ref[...] = dot(out_w[...], attn_adj, 1, 1).astype(bf16)


def fixed(shape):
    return pl.BlockSpec(shape, lambda i: (0,) * len(shape), pipeline_mode=pl.Buffered(1))


def by_rows(width):
    return pl.BlockSpec((BLOCK, width), lambda i: (i, 0))


def by_rows4(width):
    return pl.BlockSpec((4, BLOCK, width), lambda i: (0, i, 0))


def by_cols(height):
    return pl.BlockSpec((height, BLOCK), lambda i: (0, i))


def mid_fwd(scale, att, x, embed, gain, shift, teacher, cot, valid, out_w, expand, reduce):
    rows = x.shape[0]
    width = expand[0].shape[1]
    shape = jax.ShapeDtypeStruct
    return pl.pallas_call(
        mid_fwd_kernel,
        grid=(rows // BLOCK,),
        in_specs=[
            pl.BlockSpec(memory_space=pltpu.SMEM), by_cols(D), by_rows(D), fixed((1, D)), fixed((1, D)),
            fixed((1, D)), by_rows(D), by_rows(D), by_rows(1), fixed((D, D)),
        ] + [fixed((D, width))] * 4 + [fixed((width, D))] * 4,
        out_specs=[
            by_rows(D), by_rows(D), by_rows4(width), by_rows4(width), by_rows(D), by_rows(D), by_rows(D),
            fixed((1, D)),
        ],
        out_shape=[
            shape((rows, D), bf16), shape((rows, D), bf16), shape((4, rows, width), bf16),
            shape((4, rows, width), f32), shape((rows, D), bf16), shape((rows, D), f32),
            shape((rows, D), f32), shape((1, D), f32),
        ],
        cost_estimate=pl.CostEstimate(flops=22_000_000_000, transcendentals=0, bytes_accessed=30_000_000),
        name="mid_fwd",
    )(scale, att, x, embed, gain, shift, teacher, cot, valid, out_w, *expand, *reduce)


def mid_bwd(branch, slope, middle, adj, gain, out_w, expand, reduce):
    rows = branch.shape[0]
    width = expand[0].shape[1]
    shape = jax.ShapeDtypeStruct
    return pl.pallas_call(
        mid_bwd_kernel,
        grid=(rows // BLOCK,),
        in_specs=[by_rows(D), by_rows4(width), by_rows(D), by_rows(D), fixed((1, D)), fixed((D, D))]
        + [fixed((D, width))] * 4 + [fixed((width, D))] * 4,
        out_specs=[by_rows4(width), by_rows(D), by_rows(D), by_cols(D), fixed((1, D)), fixed((1, D))],
        out_shape=[
            shape((4, rows, width), bf16), shape((rows, D), f32), shape((rows, D), bf16),
            shape((D, rows), bf16), shape((1, D), f32), shape((1, D), f32),
        ],
        cost_estimate=pl.CostEstimate(flops=22_000_000_000, transcendentals=0, bytes_accessed=30_000_000),
        name="mid_bwd",
    )(branch, slope, middle, adj, gain, out_w, *expand, *reduce)


def swap(x, bit, axis="tensor"):
    size = lax.axis_size(axis)
    return lax.ppermute(x, axis, [(i, i ^ bit) for i in range(size)])


def sum_small(x, axis):
    for shift, members in levels(axis):
        x = sum((swap(x, j << shift, axis) for j in range(1, members)), x)
    return x


def levels(axis):
    steps, shift, size = [], 0, lax.axis_size(axis)
    while 1 << shift < size:
        members = 2 if shift == 0 or size >> shift < 4 else 4
        steps.append((shift, members))
        shift += members.bit_length() - 1
    return steps


def sum_scatter(x, axis):
    for shift, members in levels(axis):
        digit = (lax.axis_index(axis) >> shift) & (members - 1)
        x = x.reshape(members, x.shape[0] // members, x.shape[1])
        total = lax.dynamic_index_in_dim(x, digit, 0, False)
        for j in range(1, members):
            sent = lax.dynamic_index_in_dim(x, digit ^ j, 0, False).astype(bf16)
            total = total + swap(sent, j << shift, axis).astype(f32)
        x = total
    return x.astype(bf16)


def spread(x, axis):
    for shift, members in reversed(levels(axis)):
        digit = (lax.axis_index(axis) >> shift) & (members - 1)
        parts = [x] + [swap(x, j << shift, axis) for j in range(1, members)]
        rows = []
        for i in range(members):
            row = parts[0]
            for j in range(1, members):
                row = jnp.where(digit ^ j == i, parts[j], row)
            rows.append(row)
        x = jnp.concatenate(rows, 0)
    return x.astype(f32)


def sum_all(x, axis):
    return spread(sum_scatter(x, axis), axis)


def gather4(x):
    far = swap(x, 2)
    near = swap(x, 1)
    return [x, near, far, swap(far, 1)]


def scatter4(parts):
    near3 = swap(parts[3], 1)
    near1 = swap(parts[1], 1)
    across = (parts[2].astype(f32) + near3.astype(f32)).astype(bf16)
    mine = parts[0].astype(f32) + near1.astype(f32)
    return mine + swap(across, 2).astype(f32)


def layer(
    layer_input,
    out_cotangent,
    teacher,
    valid_mask,
    prompt_docs,
    pass_embed,
    first_gain,
    first_shift,
    project_in,
    project_out,
    second_gain,
    second_shift,
    expand_weight,
    reduce_weight,
):
    rows = layer_input.shape[0]
    width = project_out.shape[0]
    heads = width // HD
    t = lax.axis_index("tensor")
    slots = [t ^ k for k in range(4)]
    valid = valid_mask[0]
    docs = prompt_docs[0]
    valid_total = sum_small(jnp.sum(valid).astype(f32).reshape(1, 1), "dp")[0, 0]
    divisor = valid_total * D
    doc_start = jnp.zeros_like(docs)
    for v in range(3):
        doc_start = doc_start + jnp.where(docs > v, jnp.sum((docs == v).astype(jnp.int32)), 0)
    edges = jnp.arange(CONT, PROMPT + 1, CONT, dtype=jnp.int32)
    last_block = (jnp.sum((doc_start[None, :] < edges[:, None]).astype(jnp.int32), 1) + CONT - 1) // CONT
    doc_start = doc_start[None, :]
    key_bias = jnp.broadcast_to(jnp.where(valid == 1, 0.0, NEG).astype(f32)[:, None], (GLEN - PROMPT, 128))
    row_valid = lax.dynamic_slice_in_dim(
        jnp.concatenate([jnp.zeros((PROMPT,), f32), valid.astype(f32)]), t * rows, rows
    )[:, None]

    hidden_in = layer_input.astype(f32) + pass_embed
    first_affine = affine_norm(hidden_in, first_gain, first_shift)
    first_blocks = gather4(first_affine.astype(bf16))
    in_matrix = project_in.reshape(D, 3 * width)

    expand_weight, reduce_weight, project_out, _ = lax.optimization_barrier(
        (expand_weight, reduce_weight, project_out, first_blocks[2])
    )
    out_blocks = gather4(project_out)
    expand_blocks = gather4(expand_weight)
    reduce_blocks = gather4(reduce_weight)
    out_full = jnp.concatenate(out_blocks, 0)

    qkv = jnp.zeros((3 * width, GLEN), bf16)
    for k in range(4):
        part = dot(in_matrix, first_blocks[k], 0, 1).astype(bf16)
        part = jnp.concatenate([part[:width] * SCALE, part[width:]], 0)
        qkv = lax.dynamic_update_slice(qkv, part, (0, slots[k] * rows))
    qkv = qkv.reshape(3 * heads, HD, GLEN)
    saved = []
    for h in range(heads):
        saved.append(attn_fwd(h, qkv, doc_start, key_bias))
    groups = [saved[:-1], saved[-1:]]
    moved = []
    for group in groups:
        att = jnp.concatenate([x[0][0] for x in group], 0)
        cut = lambda k: lax.dynamic_slice(att, (0, slots[k] * rows), (att.shape[0], rows))
        got = {k: swap(cut(k), k) for k in (3, 2, 1)}
        got[0] = cut(0)
        moved.append(got)
    att_own = jnp.concatenate([got[k] for k in range(4) for got in moved], 0)
    layer_out, second_norm, acts, slope, branch_adj, middle, out_adj, squares = mid_fwd(
        (2.0 / divisor).reshape(1, 1), att_own, layer_input, pass_embed[None], second_gain[None],
        second_shift[None], teacher, out_cotangent, row_valid, out_full, expand_blocks, reduce_blocks,
    )
    reduce_parts = [dot(acts[k], branch_adj, 0, 0).astype(bf16) for k in range(4)]
    branch_adj, *reduce_parts = lax.optimization_barrier((branch_adj, *reduce_parts))
    reduce_grad = sum_all(scatter4(reduce_parts), "dp")
    pre_adjs, middle_adj, attn_adj, att_adj, second_gain_part, second_shift_part = mid_bwd(
        branch_adj, slope, middle, out_adj, second_gain[None], out_full, expand_blocks, reduce_blocks
    )
    att_adj = att_adj.reshape(4, heads, HD, rows)
    adj_heads = []
    for first, last in ((0, 1), (1, heads)):
        full = jnp.zeros(((last - first) * HD, GLEN), bf16)
        for k in (3, 2, 1, 0):
            piece = att_adj[k, first:last].reshape((last - first) * HD, rows)
            piece = swap(piece, k) if k else piece
            full = lax.dynamic_update_slice(full, piece, (0, slots[k] * rows))
        adj_heads += [full[h * HD : (h + 1) * HD][None] for h in range(last - first)]

    expand_parts = [dot(second_norm, pre_adjs[k], 0, 0).astype(bf16) for k in range(4)]
    out_parts = dot(att_own, attn_adj, 1, 0).astype(bf16)
    other_parts = [
        jnp.concatenate([expand_parts[k], out_parts[k * width : (k + 1) * width]], 0) for k in range(4)
    ]
    adj_heads[0], *other_parts = lax.optimization_barrier((adj_heads[0], *other_parts))
    other_grad = sum_all(scatter4(other_parts), "dp")

    proj_adj = None
    for h in range(heads):
        proj_adj = attn_bwd(h, proj_adj, last_block, qkv, adj_heads[h], *saved[h][1:], doc_start, key_bias)
    proj_adj = proj_adj.reshape(3 * width, GLEN)
    pieces = [lax.dynamic_slice(proj_adj, (0, slots[k] * rows), (3 * width, rows)) for k in range(4)]
    first_parts = []
    for k in range(4):
        first_parts.append(dot(pieces[k], in_matrix, 0, 1).astype(bf16))
    near3 = swap(first_parts[3], 1)
    near1 = swap(first_parts[1], 1)
    across = (first_parts[2].astype(f32) + near3.astype(f32)).astype(bf16)
    far = swap(across, 2)
    in_proj_grad = dot(first_blocks[0], pieces[0], 0, 1)
    for k in range(1, 4):
        in_proj_grad = in_proj_grad + dot(first_blocks[k], pieces[k], 0, 1)
    in_proj_grad = sum_all(in_proj_grad, "dp")
    input_gradient, embed_part, first_gain_part, first_shift_part = final(
        layer_input, pass_embed[None], first_gain[None], first_parts[0], near1, far, middle_adj
    )
    small = jnp.stack(
        [
            embed_part[0],
            first_gain_part[0],
            first_shift_part[0],
            second_gain_part[0],
            second_shift_part[0],
            squares[0],
        ]
    )
    small = sum_small(sum_small(small, "tensor"), "dp")
    return (
        layer_out,
        jnp.sum(small[5]) / divisor,
        input_gradient,
        small[0],
        small[1],
        small[2],
        in_proj_grad.reshape(D, 3, width),
        other_grad[D:],
        small[3],
        small[4],
        other_grad[:D],
        reduce_grad,
    )


def final_kernel(
    x_ref, embed_ref, gain_ref, part_ref, near_ref, far_ref, adj_ref, out_ref, embed_out, gain_out, shift_out
):
    norm, rstd = row_norm(x_ref[...].astype(f32) + embed_ref[...])
    first = part_ref[...].astype(f32) + near_ref[...].astype(f32) + far_ref[...].astype(f32)
    input_adj = adj_ref[...] + norm_pull(norm, rstd, first * gain_ref[...])
    out_ref[...] = input_adj.astype(bf16)

    @pl.when(pl.program_id(0) == 0)
    def _():
        embed_out[...] = jnp.zeros_like(embed_out)
        gain_out[...] = jnp.zeros_like(gain_out)
        shift_out[...] = jnp.zeros_like(shift_out)

    embed_out[...] += jnp.sum(input_adj, axis=0, keepdims=True)
    gain_out[...] += jnp.sum(first * norm, axis=0, keepdims=True)
    shift_out[...] += jnp.sum(first, axis=0, keepdims=True)


def final(x, embed, gain, part, near, far, adj):
    rows = x.shape[0]
    line = jax.ShapeDtypeStruct((1, D), f32)
    return pl.pallas_call(
        final_kernel,
        grid=(rows // BLOCK,),
        in_specs=[by_rows(D), fixed((1, D)), fixed((1, D))] + [by_rows(D)] * 4,
        out_specs=[by_rows(D)] + [fixed((1, D))] * 3,
        out_shape=[jax.ShapeDtypeStruct((rows, D), bf16), line, line, line],
        name="final",
    )(x, embed, gain, part, near, far, adj)


def solution(mesh):
    rows = P(("dp", "tensor"), None)
    return jax.shard_map(
        layer,
        mesh=mesh,
        in_specs=(
            rows,
            rows,
            rows,
            P("dp", None),
            P("dp", None),
            P(),
            P(),
            P(),
            P(None, None, "tensor"),
            P("tensor", None),
            P(),
            P(),
            P(None, "tensor"),
            P("tensor", None),
        ),
        out_specs=(
            rows,
            P(),
            rows,
            P(),
            P(),
            P(),
            P(None, None, "tensor"),
            P("tensor", None),
            P(),
            P(),
            P(None, "tensor"),
            P("tensor", None),
        ),
        check_vma=False,
    )
```

```python
import jax
import jax.numpy as jnp
from jax import lax
from jax.experimental import pallas as pl
from jax.experimental.pallas import tpu as pltpu
from jax.sharding import PartitionSpec as P


D = 768
H = 12
HD = D // H
PROMPT = 2048
CONT = 256
CONTS = 8
GLEN = 4096
DOC_MAX = 1024
NEG = -1e30
SCALE = HD ** (-0.5)
norm_eps = 1e-05
bf16 = jnp.bfloat16
f32 = jnp.float32


def dot_f32(a, b):
    return jnp.dot(a, b, preferred_element_type=f32)


def split3(x):
    high = x.astype(bf16)
    rest = x - high.astype(f32)
    middle = rest.astype(bf16)
    return high, middle, (rest - middle.astype(f32)).astype(bf16)


def fwd_kernel(q_ref, k_ref, v_ref, start_ref, bias_ref, o_ref, wide_ref, lse_ref, keys_ref, sa_ref, sb_ref):
    keys_ref[...] = k_ref[0].T
    key_ids = lax.broadcasted_iota(jnp.int32, (CONT, CONT), 0)
    row_ids = lax.broadcasted_iota(jnp.int32, (CONT, CONT), 1)
    causal = key_ids <= row_ids
    prompts = PROMPT // CONT

    def cont_keys(c):
        return [(j * CONT, None) for j in range(prompts)] + [
            (pl.multiple_of(PROMPT + c * CONT, CONT), "own")
        ]

    def scores(off, key_off, kind, c):
        s = dot_f32(keys_ref[pl.ds(key_off, CONT), :], q_ref[0, :, pl.ds(off, CONT)])
        if kind == "own":
            bias = bias_ref[pl.ds(pl.multiple_of(c * CONT, CONT), CONT), :]
            s = jnp.where(causal, s + jnp.concatenate([bias, bias], 1), NEG)
        if kind == "prompt":
            ids = key_ids + key_off
            s = jnp.where((ids <= row_ids + off) & (ids >= start_ref[:, off : off + CONT]), s, NEG)
        return s

    def step(ahead, s_ahead, behind, s_behind):
        parts = []
        total = acc = None
        ahead_keys = ahead[1] if ahead else []
        behind_keys = behind[1] if behind else []
        for j in range(max(len(ahead_keys), len(behind_keys))):
            if j < len(ahead_keys):
                s = scores(ahead[0], *ahead_keys[j], ahead[2])
                s_ahead[pl.ds(j * CONT, CONT), :] = s
                parts.append(jnp.max(s.reshape(CONT // 8, 8, CONT), 0))
            if j < len(behind_keys):
                p = jnp.exp(s_behind[pl.ds(j * CONT, CONT), :] - behind[3])
                t = jnp.sum(p.reshape(CONT // 8, 8, CONT), 0)
                o = dot_f32(v_ref[0, :, pl.ds(behind_keys[j][0], CONT)], p.astype(bf16))
                total = t if total is None else total + t
                acc = o if acc is None else acc + o
        if behind:
            off, top = behind[0], behind[3]
            total = jnp.sum(total, 0, keepdims=True)
            out = acc / total
            wide_ref[0, :, pl.ds(off, CONT)] = out
            o_ref[0, :, pl.ds(off, CONT)] = out.astype(bf16)
            lse_ref[0, :, pl.ds(off, CONT)] = top + jnp.log(total)
        if ahead:
            top = parts[0]
            for x in parts[1:]:
                top = jnp.maximum(top, x)
            return jnp.max(top, 0, keepdims=True)

    def cont(c):
        return pl.multiple_of(PROMPT + c * CONT, CONT), cont_keys(c), c

    def pair(i, top):
        c = 2 * i
        top1 = step(cont(c + 1), sb_ref, (*cont(c), top), sa_ref)
        return step(cont(c + 2), sa_ref, (*cont(c + 1), top1), sb_ref)

    top = step(cont(0), sa_ref, None, None)
    top = lax.fori_loop(0, CONTS // 2 - 1, pair, top)
    c = CONTS - 2
    top1 = step(cont(c + 1), sb_ref, (*cont(c), top), sa_ref)
    behind, refs = (*cont(c + 1), top1), (sb_ref, sa_ref)
    for i in reversed(range(prompts)):
        off = i * CONT
        keys = [(k, "prompt") for k in range(max(0, off - DOC_MAX), off + CONT, CONT)]
        top = step((off, keys, 0), refs[1], behind, refs[0])
        behind, refs = (off, keys, 0, top), refs[::-1]
    step(None, None, behind, refs[0])


def head_spec(row):
    return pl.BlockSpec((1, HD, GLEN), lambda i: (row, 0, 0))


def whole(*shape):
    return pl.BlockSpec(shape, lambda i: (0,) * len(shape))


def attn_fwd(head, qkv, doc_start, key_bias):
    heads = qkv.shape[0] // 3
    return pl.pallas_call(
        fwd_kernel,
        grid=(1,),
        in_specs=[
            head_spec(head),
            head_spec(head + heads),
            head_spec(head + 2 * heads),
            whole(1, PROMPT),
            whole(GLEN - PROMPT, 128),
        ],
        out_specs=[whole(1, HD, GLEN), whole(1, HD, GLEN), whole(1, 1, GLEN)],
        out_shape=[
            jax.ShapeDtypeStruct((1, HD, GLEN), bf16),
            jax.ShapeDtypeStruct((1, HD, GLEN), f32),
            jax.ShapeDtypeStruct((1, 1, GLEN), f32),
        ],
        scratch_shapes=[
            pltpu.VMEM((GLEN, HD), bf16),
            pltpu.VMEM((PROMPT + CONT, CONT), f32),
            pltpu.VMEM((PROMPT + CONT, CONT), f32),
        ],
        cost_estimate=pl.CostEstimate(flops=17_000_000_000, transcendentals=0, bytes_accessed=4_000_000),
        name="attn_fwd",
    )(qkv, qkv, qkv, doc_start, key_bias)


SMEM_SPEC = pl.BlockSpec(memory_space=pltpu.SMEM)
KEYS = 512
SPAN = 1024


def bwd_kernel(
    last_ref, q_ref, k_ref, v_ref, g_ref, wide_ref, lse_ref, start_ref, bias_ref,
    out_ref, qn, kn, vn, gn, qx, gx, dq,
):
    qn[...] = q_ref[0].T
    gn[...] = g_ref[0].T
    ones = jnp.where(lax.broadcasted_iota(jnp.int32, (GLEN, HD), 1) < 3, 1.0, 0.0).astype(bf16)
    kn[:, :HD] = k_ref[0].T
    kn[:, HD:] = ones
    vn[:, :HD] = v_ref[0].T
    vn[:, HD:] = ones
    zeros = jnp.zeros((HD - 16, GLEN), bf16)
    row = lax.broadcasted_iota(jnp.int32, (16, GLEN), 0)

    def extend(ref, head, tail):
        ref[0:HD, :] = head
        a, b, c = (jnp.broadcast_to(x.astype(f32), (16, GLEN)) for x in split3(-tail))
        ref[HD : HD + 16, :] = jnp.where(
            row == 0, a, jnp.where(row == 1, b, jnp.where(row == 2, c, 0.0))
        ).astype(bf16)
        ref[HD + 16 :, :] = zeros

    extend(qx, q_ref[0], lse_ref[0])
    extend(gx, g_ref[0], jnp.sum(g_ref[0].astype(f32) * wide_ref[0], 0, keepdims=True))
    dq[...] = jnp.zeros_like(dq)

    def block(key_off, key_span, off, span, mask):
        rows = pl.ds(off, span)
        keys = pl.ds(key_off, key_span)
        s = dot_f32(kn[keys, :], qx[:, rows])
        if mask is not None:
            s = mask(s)
        p = jnp.exp(s)
        ds = (p * dot_f32(vn[keys, :], gx[:, rows])).astype(bf16)
        dv = dot_f32(p.astype(bf16), gn[rows, :])
        dk = dot_f32(ds, qn[rows, :])
        dq[:, rows] += dot_f32(k_ref[0, :, keys], ds)
        return dk, dv

    def emit(key_off, key_span, dk, dv):
        out_ref[1, :, pl.ds(key_off, key_span)] = dk.T.astype(bf16)
        out_ref[2, :, pl.ds(key_off, key_span)] = dv.T.astype(bf16)

    def key_block(b, carry):
        key_off = pl.multiple_of(b * KEYS, KEYS)

        def continuation(c, acc):
            off = pl.multiple_of(PROMPT + c * SPAN, SPAN)
            dk, dv = block(key_off, KEYS, off, SPAN, None)
            return acc[0] + dk, acc[1] + dv

        zero = jnp.zeros((KEYS, HD), f32)
        acc = lax.fori_loop(0, (GLEN - PROMPT) // SPAN, continuation, (zero, zero))

        def prompt(i, acc):
            off = pl.multiple_of(i * CONT, CONT)

            def mask(s):
                key_ids = key_off + lax.broadcasted_iota(jnp.int32, s.shape, 0)
                row_ids = off + lax.broadcasted_iota(jnp.int32, s.shape, 1)
                keep = (key_ids <= row_ids) & (key_ids >= start_ref[:, pl.ds(off, CONT)])
                return jnp.where(keep, s, NEG)

            dk, dv = block(key_off, KEYS, off, CONT, mask)
            return acc[0] + dk, acc[1] + dv

        first = key_off // CONT
        acc = lax.fori_loop(first, last_ref[first + KEYS // CONT - 1], prompt, acc)
        emit(key_off, KEYS, *acc)
        return carry

    lax.fori_loop(0, PROMPT // KEYS, key_block, 0)
    causal = lax.broadcasted_iota(jnp.int32, (CONT, CONT), 0) <= lax.broadcasted_iota(
        jnp.int32, (CONT, CONT), 1
    )

    def own(c, carry):
        off = pl.multiple_of(PROMPT + c * CONT, CONT)
        bias = bias_ref[pl.ds(pl.multiple_of(c * CONT, CONT), CONT), :]

        def mask(s):
            return jnp.where(causal, s + jnp.concatenate([bias, bias], 1), NEG)

        emit(off, CONT, *block(off, CONT, off, CONT, mask))
        return carry

    lax.fori_loop(0, CONTS, own, 0)
    out_ref[0] = (dq[...] * SCALE).astype(bf16)


def attn_bwd(head, grads, bounds, qkv, adj, wide, lse, doc_start, key_bias):
    heads = qkv.shape[0] // 3
    specs = [
        SMEM_SPEC,
        head_spec(head),
        head_spec(head + heads),
        head_spec(head + 2 * heads),
        whole(1, HD, GLEN),
        whole(1, HD, GLEN),
        whole(1, 1, GLEN),
        whole(1, PROMPT),
        whole(GLEN - PROMPT, 128),
    ]
    args = [bounds, qkv, qkv, qkv, adj, wide, lse, doc_start, key_bias]
    kernel = bwd_kernel
    aliases = {}
    if grads is not None:
        specs.append(pl.BlockSpec(memory_space=pl.ANY))
        aliases = {len(args): 0}
        args.append(grads)
        kernel = lambda *refs: bwd_kernel(*refs[:9], *refs[10:])
    return pl.pallas_call(
        kernel,
        grid=(1,),
        in_specs=specs,
        out_specs=pl.BlockSpec((3, None, HD, GLEN), lambda i: (0, head, 0, 0)),
        out_shape=jax.ShapeDtypeStruct((3, heads, HD, GLEN), bf16),
        scratch_shapes=[
            pltpu.VMEM((GLEN, HD), bf16),
            pltpu.VMEM((GLEN, 2 * HD), bf16),
            pltpu.VMEM((GLEN, 2 * HD), bf16),
            pltpu.VMEM((GLEN, HD), bf16),
            pltpu.VMEM((2 * HD, GLEN), bf16),
            pltpu.VMEM((2 * HD, GLEN), bf16),
            pltpu.VMEM((HD, GLEN), f32),
        ],
        input_output_aliases=aliases,
        cost_estimate=pl.CostEstimate(flops=30_000_000_000, transcendentals=0, bytes_accessed=8_000_000),
        name="attn_bwd",
    )(*args)


def normalize(values):
    centred = values - jnp.mean(values, axis=-1, keepdims=True)
    spread = jnp.mean(centred * centred, axis=-1, keepdims=True)
    return centred * lax.rsqrt(spread + norm_eps)


def affine_norm(values, norm_gain, norm_shift):
    return normalize(values) * norm_gain + norm_shift


GELU_C = 0.7978845608028654
GELU_A = 0.044715
BLOCK = 256


def dot(a, b, ca, cb):
    return lax.dot_general(a, b, (((ca,), (cb,)), ((), ())), preferred_element_type=f32)


def row_norm(values):
    centred = values - jnp.mean(values, axis=-1, keepdims=True)
    rstd = lax.rsqrt(jnp.mean(centred * centred, axis=-1, keepdims=True) + norm_eps)
    return centred * rstd, rstd


def norm_pull(norm, rstd, adj):
    first = jnp.mean(adj, axis=-1, keepdims=True)
    second = jnp.mean(adj * norm, axis=-1, keepdims=True)
    return (adj - first - norm * second) * rstd


def mid_fwd_kernel(
    scale_ref, att_ref, x_ref, embed_ref, gain_ref, shift_ref, teacher_ref, cot_ref, valid_ref,
    out_w, e0, e1, e2, e3, r0, r1, r2, r3,
    layer_ref, norm_ref, act_ref, slope_ref, branch_ref, middle_ref, adj_ref, squares_ref,
):
    hidden = x_ref[...].astype(f32) + embed_ref[...]
    middle = hidden + dot(att_ref[...], out_w[...], 0, 0)
    middle_ref[...] = middle
    normed = (row_norm(middle)[0] * gain_ref[...] + shift_ref[...]).astype(bf16)
    norm_ref[...] = normed
    total = middle
    for k, (expand, reduce) in enumerate(((e0, r0), (e1, r1), (e2, r2), (e3, r3))):
        u = dot(normed, expand[...], 1, 0)
        square = u * u
        th = jnp.tanh(GELU_C * (u + GELU_A * (u * square)))
        half = 0.5 * (1.0 + th)
        act = (u * half).astype(bf16)
        act_ref[k] = act
        slope_ref[k] = half + (0.5 * GELU_C) * u * (1.0 - th * th) * (1.0 + (3.0 * GELU_A) * square)
        total = total + dot(act, reduce[...], 1, 0)
    layer_ref[...] = total.astype(bf16)
    deviation = valid_ref[...] * (total - teacher_ref[...].astype(f32))
    out_adj = cot_ref[...].astype(f32) + scale_ref[0, 0] * deviation
    adj_ref[...] = out_adj
    branch_ref[...] = out_adj.astype(bf16)

    @pl.when(pl.program_id(0) == 0)
    def _():
        squares_ref[...] = jnp.zeros_like(squares_ref)

    squares_ref[...] += jnp.sum(deviation * deviation, axis=0, keepdims=True)


def mid_bwd_kernel(
    branch_ref, slope_ref, middle_ref, adj_ref, gain_ref, out_w, e0, e1, e2, e3, r0, r1, r2, r3,
    pre_ref, middle_adj_ref, attn_ref, att_ref, gain_out, shift_out,
):
    branch = branch_ref[...]
    second = None
    for k, (expand, reduce) in enumerate(((e0, r0), (e1, r1), (e2, r2), (e3, r3))):
        pre = (dot(branch, reduce[...], 1, 1) * slope_ref[k]).astype(bf16)
        pre_ref[k] = pre
        part = dot(pre, expand[...], 1, 1)
        second = part if second is None else second + part
    norm, rstd = row_norm(middle_ref[...])

    @pl.when(pl.program_id(0) == 0)
    def _():
        gain_out[...] = jnp.zeros_like(gain_out)
        shift_out[...] = jnp.zeros_like(shift_out)

    gain_out[...] += jnp.sum(second * norm, axis=0, keepdims=True)
    shift_out[...] += jnp.sum(second, axis=0, keepdims=True)
    middle_adj = adj_ref[...] + norm_pull(norm, rstd, second * gain_ref[...])
    middle_adj_ref[...] = middle_adj
    attn_adj = middle_adj.astype(bf16)
    attn_ref[...] = attn_adj
    att_ref[...] = dot(out_w[...], attn_adj, 1, 1).astype(bf16)


def fixed(shape):
    return pl.BlockSpec(shape, lambda i: (0,) * len(shape), pipeline_mode=pl.Buffered(1))


def by_rows(width):
    return pl.BlockSpec((BLOCK, width), lambda i: (i, 0))


def by_rows4(width):
    return pl.BlockSpec((4, BLOCK, width), lambda i: (0, i, 0))


def by_cols(height):
    return pl.BlockSpec((height, BLOCK), lambda i: (0, i))


def mid_fwd(scale, att, x, embed, gain, shift, teacher, cot, valid, out_w, expand, reduce):
    rows = x.shape[0]
    width = expand[0].shape[1]
    shape = jax.ShapeDtypeStruct
    return pl.pallas_call(
        mid_fwd_kernel,
        grid=(rows // BLOCK,),
        in_specs=[
            pl.BlockSpec(memory_space=pltpu.SMEM), by_cols(D), by_rows(D), fixed((1, D)), fixed((1, D)),
            fixed((1, D)), by_rows(D), by_rows(D), by_rows(1), fixed((D, D)),
        ] + [fixed((D, width))] * 4 + [fixed((width, D))] * 4,
        out_specs=[
            by_rows(D), by_rows(D), by_rows4(width), by_rows4(width), by_rows(D), by_rows(D), by_rows(D),
            fixed((1, D)),
        ],
        out_shape=[
            shape((rows, D), bf16), shape((rows, D), bf16), shape((4, rows, width), bf16),
            shape((4, rows, width), f32), shape((rows, D), bf16), shape((rows, D), f32),
            shape((rows, D), f32), shape((1, D), f32),
        ],
        cost_estimate=pl.CostEstimate(flops=22_000_000_000, transcendentals=0, bytes_accessed=30_000_000),
        name="mid_fwd",
    )(scale, att, x, embed, gain, shift, teacher, cot, valid, out_w, *expand, *reduce)


def mid_bwd(branch, slope, middle, adj, gain, out_w, expand, reduce):
    rows = branch.shape[0]
    width = expand[0].shape[1]
    shape = jax.ShapeDtypeStruct
    return pl.pallas_call(
        mid_bwd_kernel,
        grid=(rows // BLOCK,),
        in_specs=[by_rows(D), by_rows4(width), by_rows(D), by_rows(D), fixed((1, D)), fixed((D, D))]
        + [fixed((D, width))] * 4 + [fixed((width, D))] * 4,
        out_specs=[by_rows4(width), by_rows(D), by_rows(D), by_cols(D), fixed((1, D)), fixed((1, D))],
        out_shape=[
            shape((4, rows, width), bf16), shape((rows, D), f32), shape((rows, D), bf16),
            shape((D, rows), bf16), shape((1, D), f32), shape((1, D), f32),
        ],
        cost_estimate=pl.CostEstimate(flops=22_000_000_000, transcendentals=0, bytes_accessed=30_000_000),
        name="mid_bwd",
    )(branch, slope, middle, adj, gain, out_w, *expand, *reduce)


def swap(x, bit, axis="tensor"):
    size = lax.axis_size(axis)
    return lax.ppermute(x, axis, [(i, i ^ bit) for i in range(size)])


def sum_small(x, axis):
    for shift, members in levels(axis):
        x = sum((swap(x, j << shift, axis) for j in range(1, members)), x)
    return x


def levels(axis):
    steps, shift, size = [], 0, lax.axis_size(axis)
    while 1 << shift < size:
        members = 2 if shift == 0 or size >> shift < 4 else 4
        steps.append((shift, members))
        shift += members.bit_length() - 1
    return steps


def sum_scatter(x, axis):
    for shift, members in levels(axis):
        digit = (lax.axis_index(axis) >> shift) & (members - 1)
        x = x.reshape(members, x.shape[0] // members, x.shape[1])
        total = lax.dynamic_index_in_dim(x, digit, 0, False)
        for j in range(1, members):
            sent = lax.dynamic_index_in_dim(x, digit ^ j, 0, False).astype(bf16)
            total = total + swap(sent, j << shift, axis).astype(f32)
        x = total
    return x.astype(bf16)


def spread(x, axis):
    for shift, members in reversed(levels(axis)):
        digit = (lax.axis_index(axis) >> shift) & (members - 1)
        parts = [x] + [swap(x, j << shift, axis) for j in range(1, members)]
        rows = []
        for i in range(members):
            row = parts[0]
            for j in range(1, members):
                row = jnp.where(digit ^ j == i, parts[j], row)
            rows.append(row)
        x = jnp.concatenate(rows, 0)
    return x.astype(f32)


def sum_all(x, axis):
    return spread(sum_scatter(x, axis), axis)


def gather4(x):
    far = swap(x, 2)
    near = swap(x, 1)
    return [x, near, far, swap(far, 1)]


def scatter4(parts):
    near3 = swap(parts[3], 1)
    near1 = swap(parts[1], 1)
    across = (parts[2].astype(f32) + near3.astype(f32)).astype(bf16)
    mine = parts[0].astype(f32) + near1.astype(f32)
    return mine + swap(across, 2).astype(f32)


def layer(
    layer_input,
    out_cotangent,
    teacher,
    valid_mask,
    prompt_docs,
    pass_embed,
    first_gain,
    first_shift,
    project_in,
    project_out,
    second_gain,
    second_shift,
    expand_weight,
    reduce_weight,
):
    rows = layer_input.shape[0]
    width = project_out.shape[0]
    heads = width // HD
    t = lax.axis_index("tensor")
    slots = [t ^ k for k in range(4)]
    valid = valid_mask[0]
    docs = prompt_docs[0]
    valid_total = sum_small(jnp.sum(valid).astype(f32).reshape(1, 1), "dp")[0, 0]
    divisor = valid_total * D
    doc_start = jnp.zeros_like(docs)
    for v in range(3):
        doc_start = doc_start + jnp.where(docs > v, jnp.sum((docs == v).astype(jnp.int32)), 0)
    edges = jnp.arange(CONT, PROMPT + 1, CONT, dtype=jnp.int32)
    last_block = (jnp.sum((doc_start[None, :] < edges[:, None]).astype(jnp.int32), 1) + CONT - 1) // CONT
    doc_start = doc_start[None, :]
    key_bias = jnp.broadcast_to(jnp.where(valid == 1, 0.0, NEG).astype(f32)[:, None], (GLEN - PROMPT, 128))
    row_valid = lax.dynamic_slice_in_dim(
        jnp.concatenate([jnp.zeros((PROMPT,), f32), valid.astype(f32)]), t * rows, rows
    )[:, None]

    hidden_in = layer_input.astype(f32) + pass_embed
    first_affine = affine_norm(hidden_in, first_gain, first_shift)
    first_blocks = gather4(first_affine.astype(bf16))
    in_matrix = project_in.reshape(D, 3 * width)

    expand_weight, reduce_weight, project_out, _ = lax.optimization_barrier(
        (expand_weight, reduce_weight, project_out, first_blocks[2])
    )
    out_blocks = gather4(project_out)
    expand_blocks = gather4(expand_weight)
    reduce_blocks = gather4(reduce_weight)
    out_full = jnp.concatenate(out_blocks, 0)

    qkv = jnp.zeros((3 * width, GLEN), bf16)
    for k in range(4):
        part = dot(in_matrix, first_blocks[k], 0, 1).astype(bf16)
        part = jnp.concatenate([part[:width] * SCALE, part[width:]], 0)
        qkv = lax.dynamic_update_slice(qkv, part, (0, slots[k] * rows))
    qkv = qkv.reshape(3 * heads, HD, GLEN)
    saved = []
    for h in range(heads):
        saved.append(attn_fwd(h, qkv, doc_start, key_bias))
    groups = [saved[:-1], saved[-1:]]
    moved = []
    for group in groups:
        att = jnp.concatenate([x[0][0] for x in group], 0)
        cut = lambda k: lax.dynamic_slice(att, (0, slots[k] * rows), (att.shape[0], rows))
        got = {k: swap(cut(k), k) for k in (3, 2, 1)}
        got[0] = cut(0)
        moved.append(got)
    att_own = jnp.concatenate([got[k] for k in range(4) for got in moved], 0)
    layer_out, second_norm, acts, slope, branch_adj, middle, out_adj, squares = mid_fwd(
        (2.0 / divisor).reshape(1, 1), att_own, layer_input, pass_embed[None], second_gain[None],
        second_shift[None], teacher, out_cotangent, row_valid, out_full, expand_blocks, reduce_blocks,
    )
    reduce_parts = [dot(acts[k], branch_adj, 0, 0).astype(bf16) for k in range(4)]
    branch_adj, *reduce_parts = lax.optimization_barrier((branch_adj, *reduce_parts))
    reduce_grad = sum_all(scatter4(reduce_parts), "dp")
    pre_adjs, middle_adj, attn_adj, att_adj, second_gain_part, second_shift_part = mid_bwd(
        branch_adj, slope, middle, out_adj, second_gain[None], out_full, expand_blocks, reduce_blocks
    )
    att_adj = att_adj.reshape(4, heads, HD, rows)
    adj_heads = []
    for first, last in ((0, 1), (1, heads)):
        full = jnp.zeros(((last - first) * HD, GLEN), bf16)
        for k in (3, 2, 1, 0):
            piece = att_adj[k, first:last].reshape((last - first) * HD, rows)
            piece = swap(piece, k) if k else piece
            full = lax.dynamic_update_slice(full, piece, (0, slots[k] * rows))
        adj_heads += [full[h * HD : (h + 1) * HD][None] for h in range(last - first)]

    expand_parts = [dot(second_norm, pre_adjs[k], 0, 0).astype(bf16) for k in range(4)]
    out_parts = dot(att_own, attn_adj, 1, 0).astype(bf16)
    other_parts = [
        jnp.concatenate([expand_parts[k], out_parts[k * width : (k + 1) * width]], 0) for k in range(4)
    ]
    adj_heads[0], *other_parts = lax.optimization_barrier((adj_heads[0], *other_parts))
    other_grad = sum_all(scatter4(other_parts), "dp")

    proj_adj = None
    for h in range(heads):
        proj_adj = attn_bwd(h, proj_adj, last_block, qkv, adj_heads[h], *saved[h][1:], doc_start, key_bias)
    proj_adj = proj_adj.reshape(3 * width, GLEN)
    pieces = [lax.dynamic_slice(proj_adj, (0, slots[k] * rows), (3 * width, rows)) for k in range(4)]
    first_parts = []
    for k in range(4):
        first_parts.append(dot(pieces[k], in_matrix, 0, 1).astype(bf16))
    near3 = swap(first_parts[3], 1)
    near1 = swap(first_parts[1], 1)
    across = (first_parts[2].astype(f32) + near3.astype(f32)).astype(bf16)
    far = swap(across, 2)
    in_proj_grad = dot(first_blocks[0], pieces[0], 0, 1)
    for k in range(1, 4):
        in_proj_grad = in_proj_grad + dot(first_blocks[k], pieces[k], 0, 1)
    in_proj_grad = sum_all(in_proj_grad, "dp")
    input_gradient, embed_part, first_gain_part, first_shift_part = final(
        layer_input, pass_embed[None], first_gain[None], first_parts[0], near1, far, middle_adj
    )
    small = jnp.stack(
        [
            embed_part[0],
            first_gain_part[0],
            first_shift_part[0],
            second_gain_part[0],
            second_shift_part[0],
            squares[0],
        ]
    )
    small = sum_small(sum_small(small, "tensor"), "dp")
    return (
        layer_out,
        jnp.sum(small[5]) / divisor,
        input_gradient,
        small[0],
        small[1],
        small[2],
        in_proj_grad.reshape(D, 3, width),
        other_grad[D:],
        small[3],
        small[4],
        other_grad[:D],
        reduce_grad,
    )


def final_kernel(
    x_ref, embed_ref, gain_ref, part_ref, near_ref, far_ref, adj_ref, out_ref, embed_out, gain_out, shift_out
):
    norm, rstd = row_norm(x_ref[...].astype(f32) + embed_ref[...])
    first = part_ref[...].astype(f32) + near_ref[...].astype(f32) + far_ref[...].astype(f32)
    input_adj = adj_ref[...] + norm_pull(norm, rstd, first * gain_ref[...])
    out_ref[...] = input_adj.astype(bf16)

    @pl.when(pl.program_id(0) == 0)
    def _():
        embed_out[...] = jnp.zeros_like(embed_out)
        gain_out[...] = jnp.zeros_like(gain_out)
        shift_out[...] = jnp.zeros_like(shift_out)

    embed_out[...] += jnp.sum(input_adj, axis=0, keepdims=True)
    gain_out[...] += jnp.sum(first * norm, axis=0, keepdims=True)
    shift_out[...] += jnp.sum(first, axis=0, keepdims=True)


def final(x, embed, gain, part, near, far, adj):
    rows = x.shape[0]
    line = jax.ShapeDtypeStruct((1, D), f32)
    return pl.pallas_call(
        final_kernel,
        grid=(rows // BLOCK,),
        in_specs=[by_rows(D), fixed((1, D)), fixed((1, D))] + [by_rows(D)] * 4,
        out_specs=[by_rows(D)] + [fixed((1, D))] * 3,
        out_shape=[jax.ShapeDtypeStruct((rows, D), bf16), line, line, line],
        name="final",
    )(x, embed, gain, part, near, far, adj)


def solution(mesh):
    rows = P(("dp", "tensor"), None)
    return jax.shard_map(
        layer,
        mesh=mesh,
        in_specs=(
            rows,
            rows,
            rows,
            P("dp", None),
            P("dp", None),
            P(),
            P(),
            P(),
            P(None, None, "tensor"),
            P("tensor", None),
            P(),
            P(),
            P(None, "tensor"),
            P("tensor", None),
        ),
        out_specs=(
            rows,
            P(),
            rows,
            P(),
            P(),
            P(),
            P(None, None, "tensor"),
            P("tensor", None),
            P(),
            P(),
            P(None, "tensor"),
            P("tensor", None),
        ),
        check_vma=False,
    )
```

```python
import jax
import jax.numpy as jnp
from jax import lax
from jax.experimental import pallas as pl
from jax.experimental.pallas import tpu as pltpu
from jax.sharding import PartitionSpec as P


D = 768
H = 12
HD = D // H
PROMPT = 2048
CONT = 256
CONTS = 8
GLEN = 4096
DOC_MAX = 1024
NEG = -1e30
SCALE = HD ** (-0.5)
norm_eps = 1e-05
bf16 = jnp.bfloat16
f32 = jnp.float32


def dot_f32(a, b):
    return jnp.dot(a, b, preferred_element_type=f32)


def split3(x):
    high = x.astype(bf16)
    rest = x - high.astype(f32)
    middle = rest.astype(bf16)
    return high, middle, (rest - middle.astype(f32)).astype(bf16)


def fwd_kernel(q_ref, k_ref, v_ref, start_ref, bias_ref, o_ref, wide_ref, lse_ref, keys_ref, sa_ref, sb_ref):
    keys_ref[...] = k_ref[0].T
    key_ids = lax.broadcasted_iota(jnp.int32, (CONT, CONT), 0)
    row_ids = lax.broadcasted_iota(jnp.int32, (CONT, CONT), 1)
    causal = key_ids <= row_ids
    prompts = PROMPT // CONT

    def cont_keys(c):
        return [(j * CONT, None) for j in range(prompts)] + [
            (pl.multiple_of(PROMPT + c * CONT, CONT), "own")
        ]

    def scores(off, key_off, kind, c):
        s = dot_f32(keys_ref[pl.ds(key_off, CONT), :], q_ref[0, :, pl.ds(off, CONT)])
        if kind == "own":
            bias = bias_ref[pl.ds(pl.multiple_of(c * CONT, CONT), CONT), :]
            s = jnp.where(causal, s + jnp.concatenate([bias, bias], 1), NEG)
        if kind == "prompt":
            ids = key_ids + key_off
            s = jnp.where((ids <= row_ids + off) & (ids >= start_ref[:, off : off + CONT]), s, NEG)
        return s

    def step(ahead, s_ahead, behind, s_behind):
        parts = []
        total = acc = None
        ahead_keys = ahead[1] if ahead else []
        behind_keys = behind[1] if behind else []
        for j in range(max(len(ahead_keys), len(behind_keys))):
            if j < len(ahead_keys):
                s = scores(ahead[0], *ahead_keys[j], ahead[2])
                s_ahead[pl.ds(j * CONT, CONT), :] = s
                parts.append(jnp.max(s.reshape(CONT // 8, 8, CONT), 0))
            if j < len(behind_keys):
                p = jnp.exp(s_behind[pl.ds(j * CONT, CONT), :] - behind[3])
                t = jnp.sum(p.reshape(CONT // 8, 8, CONT), 0)
                o = dot_f32(v_ref[0, :, pl.ds(behind_keys[j][0], CONT)], p.astype(bf16))
                total = t if total is None else total + t
                acc = o if acc is None else acc + o
        if behind:
            off, top = behind[0], behind[3]
            total = jnp.sum(total, 0, keepdims=True)
            out = acc / total
            wide_ref[0, :, pl.ds(off, CONT)] = out
            o_ref[0, :, pl.ds(off, CONT)] = out.astype(bf16)
            lse_ref[0, :, pl.ds(off, CONT)] = top + jnp.log(total)
        if ahead:
            top = parts[0]
            for x in parts[1:]:
                top = jnp.maximum(top, x)
            return jnp.max(top, 0, keepdims=True)

    def cont(c):
        return pl.multiple_of(PROMPT + c * CONT, CONT), cont_keys(c), c

    def pair(i, top):
        c = 2 * i
        top1 = step(cont(c + 1), sb_ref, (*cont(c), top), sa_ref)
        return step(cont(c + 2), sa_ref, (*cont(c + 1), top1), sb_ref)

    top = step(cont(0), sa_ref, None, None)
    top = lax.fori_loop(0, CONTS // 2 - 1, pair, top)
    c = CONTS - 2
    top1 = step(cont(c + 1), sb_ref, (*cont(c), top), sa_ref)
    behind, refs = (*cont(c + 1), top1), (sb_ref, sa_ref)
    for i in reversed(range(prompts)):
        off = i * CONT
        keys = [(k, "prompt") for k in range(max(0, off - DOC_MAX), off + CONT, CONT)]
        top = step((off, keys, 0), refs[1], behind, refs[0])
        behind, refs = (off, keys, 0, top), refs[::-1]
    step(None, None, behind, refs[0])


def head_spec(row):
    return pl.BlockSpec((1, HD, GLEN), lambda i: (row, 0, 0))


def whole(*shape):
    return pl.BlockSpec(shape, lambda i: (0,) * len(shape))


def attn_fwd(head, qkv, doc_start, key_bias):
    heads = qkv.shape[0] // 3
    return pl.pallas_call(
        fwd_kernel,
        grid=(1,),
        in_specs=[
            head_spec(head),
            head_spec(head + heads),
            head_spec(head + 2 * heads),
            whole(1, PROMPT),
            whole(GLEN - PROMPT, 128),
        ],
        out_specs=[whole(1, HD, GLEN), whole(1, HD, GLEN), whole(1, 1, GLEN)],
        out_shape=[
            jax.ShapeDtypeStruct((1, HD, GLEN), bf16),
            jax.ShapeDtypeStruct((1, HD, GLEN), f32),
            jax.ShapeDtypeStruct((1, 1, GLEN), f32),
        ],
        scratch_shapes=[
            pltpu.VMEM((GLEN, HD), bf16),
            pltpu.VMEM((PROMPT + CONT, CONT), f32),
            pltpu.VMEM((PROMPT + CONT, CONT), f32),
        ],
        cost_estimate=pl.CostEstimate(flops=17_000_000_000, transcendentals=0, bytes_accessed=4_000_000),
        name="attn_fwd",
    )(qkv, qkv, qkv, doc_start, key_bias)


SMEM_SPEC = pl.BlockSpec(memory_space=pltpu.SMEM)
KEYS = 512
SPAN = 1024


def bwd_kernel(
    last_ref, slots_ref, q_ref, k_ref, v_ref, g0, g1, g2, g3, wide_ref, lse_ref, start_ref, bias_ref,
    out_ref, qn, kn, vn, gn, qx, gx, dq,
):
    qn[...] = q_ref[0].T
    for n, piece in enumerate((g0, g1, g2, g3)):
        size = piece.shape[1]
        place = pl.ds(pl.multiple_of(slots_ref[n] * size, size), size)
        gx[0:HD, place] = piece[...]
        gn[place, :] = piece[...].T
    ones = jnp.where(lax.broadcasted_iota(jnp.int32, (GLEN, HD), 1) < 3, 1.0, 0.0).astype(bf16)
    kn[:, :HD] = k_ref[0].T
    kn[:, HD:] = ones
    vn[:, :HD] = v_ref[0].T
    vn[:, HD:] = ones
    zeros = jnp.zeros((HD - 16, GLEN), bf16)
    row = lax.broadcasted_iota(jnp.int32, (16, GLEN), 0)

    def extend(ref, tail):
        a, b, c = (jnp.broadcast_to(x.astype(f32), (16, GLEN)) for x in split3(-tail))
        ref[HD : HD + 16, :] = jnp.where(
            row == 0, a, jnp.where(row == 1, b, jnp.where(row == 2, c, 0.0))
        ).astype(bf16)
        ref[HD + 16 :, :] = zeros

    qx[0:HD, :] = q_ref[0]
    extend(qx, lse_ref[0])
    extend(gx, jnp.sum(gx[0:HD, :].astype(f32) * wide_ref[0], 0, keepdims=True))
    dq[...] = jnp.zeros_like(dq)

    def block(key_off, key_span, off, span, mask):
        rows = pl.ds(off, span)
        keys = pl.ds(key_off, key_span)
        s = dot_f32(kn[keys, :], qx[:, rows])
        if mask is not None:
            s = mask(s)
        p = jnp.exp(s)
        ds = (p * dot_f32(vn[keys, :], gx[:, rows])).astype(bf16)
        dv = dot_f32(p.astype(bf16), gn[rows, :])
        dk = dot_f32(ds, qn[rows, :])
        dq[:, rows] += dot_f32(k_ref[0, :, keys], ds)
        return dk, dv

    def emit(key_off, key_span, dk, dv):
        out_ref[1, :, pl.ds(key_off, key_span)] = dk.T.astype(bf16)
        out_ref[2, :, pl.ds(key_off, key_span)] = dv.T.astype(bf16)

    def key_block(b, carry):
        key_off = pl.multiple_of(b * KEYS, KEYS)

        def continuation(c, acc):
            off = pl.multiple_of(PROMPT + c * SPAN, SPAN)
            dk, dv = block(key_off, KEYS, off, SPAN, None)
            return acc[0] + dk, acc[1] + dv

        zero = jnp.zeros((KEYS, HD), f32)
        acc = lax.fori_loop(0, (GLEN - PROMPT) // SPAN, continuation, (zero, zero))

        def prompt(i, acc):
            off = pl.multiple_of(i * CONT, CONT)

            def mask(s):
                key_ids = key_off + lax.broadcasted_iota(jnp.int32, s.shape, 0)
                row_ids = off + lax.broadcasted_iota(jnp.int32, s.shape, 1)
                keep = (key_ids <= row_ids) & (key_ids >= start_ref[:, pl.ds(off, CONT)])
                return jnp.where(keep, s, NEG)

            dk, dv = block(key_off, KEYS, off, CONT, mask)
            return acc[0] + dk, acc[1] + dv

        first = key_off // CONT
        acc = lax.fori_loop(first, last_ref[first + KEYS // CONT - 1], prompt, acc)
        emit(key_off, KEYS, *acc)
        return carry

    lax.fori_loop(0, PROMPT // KEYS, key_block, 0)
    causal = lax.broadcasted_iota(jnp.int32, (CONT, CONT), 0) <= lax.broadcasted_iota(
        jnp.int32, (CONT, CONT), 1
    )

    def own(c, carry):
        off = pl.multiple_of(PROMPT + c * CONT, CONT)
        bias = bias_ref[pl.ds(pl.multiple_of(c * CONT, CONT), CONT), :]

        def mask(s):
            return jnp.where(causal, s + jnp.concatenate([bias, bias], 1), NEG)

        emit(off, CONT, *block(off, CONT, off, CONT, mask))
        return carry

    lax.fori_loop(0, CONTS, own, 0)
    out_ref[0] = (dq[...] * SCALE).astype(bf16)


def attn_bwd(head, grads, bounds, slots, qkv, pieces, row, wide, lse, doc_start, key_bias):
    heads = qkv.shape[0] // 3
    specs = [
        SMEM_SPEC,
        SMEM_SPEC,
        head_spec(head),
        head_spec(head + heads),
        head_spec(head + 2 * heads),
    ]
    specs += [pl.BlockSpec((HD, piece.shape[1]), lambda i: (row, 0)) for piece in pieces]
    specs += [
        whole(1, HD, GLEN),
        whole(1, 1, GLEN),
        whole(1, PROMPT),
        whole(GLEN - PROMPT, 128),
    ]
    args = [bounds, slots, qkv, qkv, qkv, *pieces, wide, lse, doc_start, key_bias]
    kernel = bwd_kernel
    aliases = {}
    if grads is not None:
        specs.append(pl.BlockSpec(memory_space=pl.ANY))
        aliases = {len(args): 0}
        args.append(grads)
        kernel = lambda *refs: bwd_kernel(*refs[:13], *refs[14:])
    return pl.pallas_call(
        kernel,
        grid=(1,),
        in_specs=specs,
        out_specs=pl.BlockSpec((3, None, HD, GLEN), lambda i: (0, head, 0, 0)),
        out_shape=jax.ShapeDtypeStruct((3, heads, HD, GLEN), bf16),
        scratch_shapes=[
            pltpu.VMEM((GLEN, HD), bf16),
            pltpu.VMEM((GLEN, 2 * HD), bf16),
            pltpu.VMEM((GLEN, 2 * HD), bf16),
            pltpu.VMEM((GLEN, HD), bf16),
            pltpu.VMEM((2 * HD, GLEN), bf16),
            pltpu.VMEM((2 * HD, GLEN), bf16),
            pltpu.VMEM((HD, GLEN), f32),
        ],
        input_output_aliases=aliases,
        cost_estimate=pl.CostEstimate(flops=30_000_000_000, transcendentals=0, bytes_accessed=8_000_000),
        name="attn_bwd",
    )(*args)


def normalize(values):
    centred = values - jnp.mean(values, axis=-1, keepdims=True)
    spread = jnp.mean(centred * centred, axis=-1, keepdims=True)
    return centred * lax.rsqrt(spread + norm_eps)


def affine_norm(values, norm_gain, norm_shift):
    return normalize(values) * norm_gain + norm_shift


GELU_C = 0.7978845608028654
GELU_A = 0.044715
BLOCK = 256


def dot(a, b, ca, cb):
    return lax.dot_general(a, b, (((ca,), (cb,)), ((), ())), preferred_element_type=f32)


def row_norm(values):
    centred = values - jnp.mean(values, axis=-1, keepdims=True)
    rstd = lax.rsqrt(jnp.mean(centred * centred, axis=-1, keepdims=True) + norm_eps)
    return centred * rstd, rstd


def norm_pull(norm, rstd, adj):
    first = jnp.mean(adj, axis=-1, keepdims=True)
    second = jnp.mean(adj * norm, axis=-1, keepdims=True)
    return (adj - first - norm * second) * rstd


def join_rows(joined, *parts):
    @pl.when(pl.program_id(0) == 0)
    def _():
        size = parts[0].shape[0]
        for k, part in enumerate(parts):
            joined[k * size : (k + 1) * size, :] = part[...]


def packed_specs(rows):
    once = pl.Buffered(1)
    expand = pl.BlockSpec((D, D), lambda i: (0, 0), pipeline_mode=once)
    reduce = pl.BlockSpec((D, D), lambda i: (1, 0), pipeline_mode=once)
    size = rows - 2 * D
    last = pl.BlockSpec((size, D), lambda i: (2 * D // size, 0), pipeline_mode=once)
    return [expand] * 4 + [reduce] * 4 + [last] * 4


def mid_fwd_kernel(
    scale_ref, a0, a1, a2, a3, b0, b1, b2, b3,
    x_ref, embed_ref, gain_ref, shift_ref, teacher_ref, cot_ref, valid_ref,
    e0, e1, e2, e3, r0, r1, r2, r3, w0, w1, w2, w3,
    layer_ref, norm_ref, act_ref, slope_ref, branch_ref, middle_ref, adj_ref, att_ref, squares_ref, out_w,
):
    join_rows(out_w, w0, w1, w2, w3)
    place = 0
    for piece in (a0, b0, a1, b1, a2, b2, a3, b3):
        att_ref[place : place + piece.shape[0], :] = piece[...]
        place += piece.shape[0]
    hidden = x_ref[...].astype(f32) + embed_ref[...]
    middle = hidden + dot(att_ref[...], out_w[...], 0, 0)
    middle_ref[...] = middle
    normed = (row_norm(middle)[0] * gain_ref[...] + shift_ref[...]).astype(bf16)
    norm_ref[...] = normed
    total = middle
    for k, (expand, reduce) in enumerate(((e0, r0), (e1, r1), (e2, r2), (e3, r3))):
        u = dot(normed, expand[...], 1, 0)
        square = u * u
        th = jnp.tanh(GELU_C * (u + GELU_A * (u * square)))
        half = 0.5 * (1.0 + th)
        act = (u * half).astype(bf16)
        act_ref[k] = act
        slope_ref[k] = half + (0.5 * GELU_C) * u * (1.0 - th * th) * (1.0 + (3.0 * GELU_A) * square)
        total = total + dot(act, reduce[...], 1, 0)
    layer_ref[...] = total.astype(bf16)
    deviation = valid_ref[...] * (total - teacher_ref[...].astype(f32))
    out_adj = cot_ref[...].astype(f32) + scale_ref[0, 0] * deviation
    adj_ref[...] = out_adj
    branch_ref[...] = out_adj.astype(bf16)

    @pl.when(pl.program_id(0) == 0)
    def _():
        squares_ref[...] = jnp.zeros_like(squares_ref)

    squares_ref[...] += jnp.sum(deviation * deviation, axis=0, keepdims=True)


def mid_bwd_kernel(
    branch_ref, slope_ref, middle_ref, adj_ref, gain_ref, e0, e1, e2, e3, r0, r1, r2, r3, w0, w1, w2, w3,
    pre_ref, middle_adj_ref, attn_ref, att_ref, gain_out, shift_out, out_w,
):
    join_rows(out_w, w0, w1, w2, w3)
    branch = branch_ref[...]
    second = None
    for k, (expand, reduce) in enumerate(((e0, r0), (e1, r1), (e2, r2), (e3, r3))):
        pre = (dot(branch, reduce[...], 1, 1) * slope_ref[k]).astype(bf16)
        pre_ref[k] = pre
        part = dot(pre, expand[...], 1, 1)
        second = part if second is None else second + part
    norm, rstd = row_norm(middle_ref[...])

    @pl.when(pl.program_id(0) == 0)
    def _():
        gain_out[...] = jnp.zeros_like(gain_out)
        shift_out[...] = jnp.zeros_like(shift_out)

    gain_out[...] += jnp.sum(second * norm, axis=0, keepdims=True)
    shift_out[...] += jnp.sum(second, axis=0, keepdims=True)
    middle_adj = adj_ref[...] + norm_pull(norm, rstd, second * gain_ref[...])
    middle_adj_ref[...] = middle_adj
    attn_adj = middle_adj.astype(bf16)
    attn_ref[...] = attn_adj
    att_ref[...] = dot(out_w[...], attn_adj, 1, 1).astype(bf16)


def fixed(shape):
    return pl.BlockSpec(shape, lambda i: (0,) * len(shape), pipeline_mode=pl.Buffered(1))


def by_rows(width):
    return pl.BlockSpec((BLOCK, width), lambda i: (i, 0))


def by_rows4(width):
    return pl.BlockSpec((4, BLOCK, width), lambda i: (0, i, 0))


def by_cols(height):
    return pl.BlockSpec((height, BLOCK), lambda i: (0, i))


def mid_fwd(scale, att, x, embed, gain, shift, teacher, cot, valid, weights):
    rows = x.shape[0]
    width = D
    shape = jax.ShapeDtypeStruct
    return pl.pallas_call(
        mid_fwd_kernel,
        grid=(rows // BLOCK,),
        in_specs=[
            pl.BlockSpec(memory_space=pltpu.SMEM),
        ] + [by_cols(piece.shape[0]) for piece in att] + [
            by_rows(D), fixed((1, D)), fixed((1, D)),
            fixed((1, D)), by_rows(D), by_rows(D), by_rows(1),
        ] + packed_specs(weights[0].shape[0]),
        out_specs=[
            by_rows(D), by_rows(D), by_rows4(width), by_rows4(width), by_rows(D), by_rows(D), by_rows(D),
            by_cols(D), fixed((1, D)),
        ],
        out_shape=[
            shape((rows, D), bf16), shape((rows, D), bf16), shape((4, rows, width), bf16),
            shape((4, rows, width), f32), shape((rows, D), bf16), shape((rows, D), f32),
            shape((rows, D), f32), shape((D, rows), bf16), shape((1, D), f32),
        ],
        cost_estimate=pl.CostEstimate(flops=22_000_000_000, transcendentals=0, bytes_accessed=30_000_000),
        scratch_shapes=[pltpu.VMEM((D, D), bf16)],
        name="mid_fwd",
    )(scale, *att, x, embed, gain, shift, teacher, cot, valid, *weights, *weights, *weights)


def mid_bwd(branch, slope, middle, adj, gain, weights):
    rows = branch.shape[0]
    width = D
    shape = jax.ShapeDtypeStruct
    return pl.pallas_call(
        mid_bwd_kernel,
        grid=(rows // BLOCK,),
        in_specs=[by_rows(D), by_rows4(width), by_rows(D), by_rows(D), fixed((1, D))]
        + packed_specs(weights[0].shape[0]),
        out_specs=[by_rows4(width), by_rows(D), by_rows(D), by_cols(D), fixed((1, D)), fixed((1, D))],
        out_shape=[
            shape((4, rows, width), bf16), shape((rows, D), f32), shape((rows, D), bf16),
            shape((D, rows), bf16), shape((1, D), f32), shape((1, D), f32),
        ],
        cost_estimate=pl.CostEstimate(flops=22_000_000_000, transcendentals=0, bytes_accessed=30_000_000),
        scratch_shapes=[pltpu.VMEM((D, D), bf16)],
        name="mid_bwd",
    )(branch, slope, middle, adj, gain, *weights, *weights, *weights)


def swap(x, bit, axis="tensor"):
    size = lax.axis_size(axis)
    return lax.ppermute(x, axis, [(i, i ^ bit) for i in range(size)])


def sum_small(x, axis):
    for shift, members in levels(axis):
        x = sum((swap(x, j << shift, axis) for j in range(1, members)), x)
    return x


def levels(axis):
    steps, shift, size = [], 0, lax.axis_size(axis)
    while 1 << shift < size:
        members = 2 if shift == 0 or size >> shift < 4 else 4
        steps.append((shift, members))
        shift += members.bit_length() - 1
    return steps


def sum_scatter(x, axis):
    for shift, members in levels(axis):
        digit = (lax.axis_index(axis) >> shift) & (members - 1)
        x = x.reshape(members, x.shape[0] // members, x.shape[1])
        total = lax.dynamic_index_in_dim(x, digit, 0, False)
        for j in range(1, members):
            sent = lax.dynamic_index_in_dim(x, digit ^ j, 0, False).astype(bf16)
            total = total + swap(sent, j << shift, axis).astype(f32)
        x = total
    return x.astype(bf16)


def spread(x, axis):
    for shift, members in reversed(levels(axis)):
        digit = (lax.axis_index(axis) >> shift) & (members - 1)
        parts = [x] + [swap(x, j << shift, axis) for j in range(1, members)]
        rows = []
        for i in range(members):
            row = parts[0]
            for j in range(1, members):
                row = jnp.where(digit ^ j == i, parts[j], row)
            rows.append(row)
        x = jnp.concatenate(rows, 0)
    return x.astype(f32)


def sum_all(x, axis):
    return spread(sum_scatter(x, axis), axis)


def gather4(x):
    far = swap(x, 2)
    near = swap(x, 1)
    return [x, near, far, swap(far, 1)]


def scatter4(parts):
    near3 = swap(parts[3], 1)
    near1 = swap(parts[1], 1)
    across = (parts[2].astype(f32) + near3.astype(f32)).astype(bf16)
    mine = parts[0].astype(f32) + near1.astype(f32)
    return mine + swap(across, 2).astype(f32)


def layer(
    layer_input,
    out_cotangent,
    teacher,
    valid_mask,
    prompt_docs,
    pass_embed,
    first_gain,
    first_shift,
    project_in,
    project_out,
    second_gain,
    second_shift,
    expand_weight,
    reduce_weight,
):
    rows = layer_input.shape[0]
    width = project_out.shape[0]
    heads = width // HD
    t = lax.axis_index("tensor")
    slots = [t ^ k for k in range(4)]
    valid = valid_mask[0]
    docs = prompt_docs[0]
    valid_total = sum_small(jnp.sum(valid).astype(f32).reshape(1, 1), "dp")[0, 0]
    doc_start = jnp.zeros_like(docs)
    for v in range(3):
        doc_start = doc_start + jnp.where(docs > v, jnp.sum((docs == v).astype(jnp.int32)), 0)
    edges = jnp.arange(CONT, PROMPT + 1, CONT, dtype=jnp.int32)
    last_block = (jnp.sum((doc_start[None, :] < edges[:, None]).astype(jnp.int32), 1) + CONT - 1) // CONT
    doc_start = doc_start[None, :]
    key_bias = jnp.broadcast_to(jnp.where(valid == 1, 0.0, NEG).astype(f32)[:, None], (GLEN - PROMPT, 128))
    row_valid = lax.dynamic_slice_in_dim(
        jnp.concatenate([jnp.zeros((PROMPT,), f32), valid.astype(f32)]), t * rows, rows
    )[:, None]

    hidden_in = layer_input.astype(f32) + pass_embed
    first_affine = affine_norm(hidden_in, first_gain, first_shift)
    first_norm = first_affine.astype(bf16)
    far = swap(first_norm, 2)
    near = swap(first_norm, 1)
    in_matrix = project_in.reshape(D, 3 * width)

    def project(block):
        part = dot(in_matrix, block, 0, 1).astype(bf16)
        return jnp.concatenate([part[:width] * SCALE, part[width:]], 0)

    qkv = lax.dynamic_update_slice(jnp.zeros((3 * width, GLEN), bf16), project(first_norm), (0, slots[0] * rows))
    far, valid_total, qkv = lax.optimization_barrier((far, valid_total, qkv))
    divisor = valid_total * D
    first_blocks = [first_norm, near, far, swap(far, 1)]
    packed = jnp.concatenate([expand_weight, reduce_weight, project_out], 0)
    packed, _ = lax.optimization_barrier((packed, far))
    weights = gather4(packed)

    for k in range(1, 4):
        qkv = lax.dynamic_update_slice(qkv, project(first_blocks[k]), (0, slots[k] * rows))
    qkv = qkv.reshape(3 * heads, HD, GLEN)
    saved = []
    for h in range(heads):
        saved.append(attn_fwd(h, qkv, doc_start, key_bias))
    groups = [saved[:-1], saved[-1:]]
    moved = []
    for group in groups:
        att = jnp.concatenate([x[0][0] for x in group], 0)
        cut = lambda k: lax.dynamic_slice(att, (0, slots[k] * rows), (att.shape[0], rows))
        got = {k: swap(cut(k), k) for k in (3, 2, 1)}
        got[0] = cut(0)
        moved.append(got)
    att_pieces = [got[k] for got in moved for k in range(4)]
    layer_out, second_norm, acts, slope, branch_adj, middle, out_adj, att_own, squares = mid_fwd(
        (2.0 / divisor).reshape(1, 1), att_pieces, layer_input, pass_embed[None], second_gain[None],
        second_shift[None], teacher, out_cotangent, row_valid, weights,
    )
    reduce_parts = [dot(acts[k], branch_adj, 0, 0).astype(bf16) for k in range(4)]
    branch_adj, *reduce_parts = lax.optimization_barrier((branch_adj, *reduce_parts))
    reduce_grad = sum_all(scatter4(reduce_parts), "dp")
    pre_adjs, middle_adj, attn_adj, att_adj, second_gain_part, second_shift_part = mid_bwd(
        branch_adj, slope, middle, out_adj, second_gain[None], weights
    )
    att_adj = att_adj.reshape(4, heads, HD, rows)
    adj_heads = []
    for first, last in ((0, 1), (1, heads)):
        pieces = [None] * 4
        for k in (3, 2, 1, 0):
            piece = att_adj[k, first:last].reshape((last - first) * HD, rows)
            pieces[k] = swap(piece, k) if k else piece
        adj_heads += [(pieces, h) for h in range(last - first)]

    expand_parts = [dot(second_norm, pre_adjs[k], 0, 0).astype(bf16) for k in range(4)]
    out_parts = dot(att_own, attn_adj, 1, 0).astype(bf16)
    other_parts = [
        jnp.concatenate([expand_parts[k], out_parts[k * width : (k + 1) * width]], 0) for k in range(4)
    ]
    own, *other_parts = lax.optimization_barrier((adj_heads[0][0][0], *other_parts))
    adj_heads[0][0][0] = own
    other_grad = sum_all(scatter4(other_parts), "dp")

    proj_adj = None
    for h in range(heads):
        proj_adj = attn_bwd(h, proj_adj, last_block, jnp.stack(slots), qkv, *adj_heads[h], *saved[h][1:], doc_start, key_bias)
    proj_adj = proj_adj.reshape(3 * width, GLEN)
    pieces = [lax.dynamic_slice(proj_adj, (0, slots[k] * rows), (3 * width, rows)) for k in range(4)]
    first_parts = []
    for k in range(4):
        first_parts.append(dot(pieces[k], in_matrix, 0, 1).astype(bf16))
    near3 = swap(first_parts[3], 1)
    near1 = swap(first_parts[1], 1)
    across = (first_parts[2].astype(f32) + near3.astype(f32)).astype(bf16)
    far = swap(across, 2)
    in_proj_grad = dot(first_blocks[0], pieces[0], 0, 1)
    for k in range(1, 4):
        in_proj_grad = in_proj_grad + dot(first_blocks[k], pieces[k], 0, 1)
    in_proj_grad = sum_all(in_proj_grad, "dp")
    input_gradient, embed_part, first_gain_part, first_shift_part = final(
        layer_input, pass_embed[None], first_gain[None], first_parts[0], near1, far, middle_adj
    )
    small = jnp.stack(
        [
            embed_part[0],
            first_gain_part[0],
            first_shift_part[0],
            second_gain_part[0],
            second_shift_part[0],
            squares[0],
        ]
    )
    small = sum_small(sum_small(small, "tensor"), "dp")
    return (
        layer_out,
        jnp.sum(small[5]) / divisor,
        input_gradient,
        small[0],
        small[1],
        small[2],
        in_proj_grad.reshape(D, 3, width),
        other_grad[D:],
        small[3],
        small[4],
        other_grad[:D],
        reduce_grad,
    )


def final_kernel(
    x_ref, embed_ref, gain_ref, part_ref, near_ref, far_ref, adj_ref, out_ref, embed_out, gain_out, shift_out
):
    norm, rstd = row_norm(x_ref[...].astype(f32) + embed_ref[...])
    first = part_ref[...].astype(f32) + near_ref[...].astype(f32) + far_ref[...].astype(f32)
    input_adj = adj_ref[...] + norm_pull(norm, rstd, first * gain_ref[...])
    out_ref[...] = input_adj.astype(bf16)

    @pl.when(pl.program_id(0) == 0)
    def _():
        embed_out[...] = jnp.zeros_like(embed_out)
        gain_out[...] = jnp.zeros_like(gain_out)
        shift_out[...] = jnp.zeros_like(shift_out)

    embed_out[...] += jnp.sum(input_adj, axis=0, keepdims=True)
    gain_out[...] += jnp.sum(first * norm, axis=0, keepdims=True)
    shift_out[...] += jnp.sum(first, axis=0, keepdims=True)


def final(x, embed, gain, part, near, far, adj):
    rows = x.shape[0]
    line = jax.ShapeDtypeStruct((1, D), f32)
    return pl.pallas_call(
        final_kernel,
        grid=(rows // BLOCK,),
        in_specs=[by_rows(D), fixed((1, D)), fixed((1, D))] + [by_rows(D)] * 4,
        out_specs=[by_rows(D)] + [fixed((1, D))] * 3,
        out_shape=[jax.ShapeDtypeStruct((rows, D), bf16), line, line, line],
        name="final",
    )(x, embed, gain, part, near, far, adj)


def solution(mesh):
    rows = P(("dp", "tensor"), None)
    return jax.shard_map(
        layer,
        mesh=mesh,
        in_specs=(
            rows,
            rows,
            rows,
            P("dp", None),
            P("dp", None),
            P(),
            P(),
            P(),
            P(None, None, "tensor"),
            P("tensor", None),
            P(),
            P(),
            P(None, "tensor"),
            P("tensor", None),
        ),
        out_specs=(
            rows,
            P(),
            rows,
            P(),
            P(),
            P(),
            P(None, None, "tensor"),
            P("tensor", None),
            P(),
            P(),
            P(None, "tensor"),
            P("tensor", None),
        ),
        check_vma=False,
    )
```

```python
import jax
import jax.numpy as jnp
from jax import lax
from jax.experimental import pallas as pl
from jax.experimental.pallas import tpu as pltpu
from jax.sharding import PartitionSpec as P


D = 768
H = 12
HD = D // H
PROMPT = 2048
CONT = 256
CONTS = 8
GLEN = 4096
DOC_MAX = 1024
NEG = -1e30
SCALE = HD ** (-0.5)
norm_eps = 1e-05
bf16 = jnp.bfloat16
f32 = jnp.float32


def dot_f32(a, b):
    return jnp.dot(a, b, preferred_element_type=f32)


def split3(x):
    high = x.astype(bf16)
    rest = x - high.astype(f32)
    middle = rest.astype(bf16)
    return high, middle, (rest - middle.astype(f32)).astype(bf16)


def fwd_kernel(q_ref, k_ref, v_ref, start_ref, bias_ref, o_ref, wide_ref, lse_ref, keys_ref, sa_ref, sb_ref):
    keys_ref[...] = k_ref[0].T
    key_ids = lax.broadcasted_iota(jnp.int32, (CONT, CONT), 0)
    row_ids = lax.broadcasted_iota(jnp.int32, (CONT, CONT), 1)
    causal = key_ids <= row_ids
    prompts = PROMPT // CONT

    def cont_keys(c):
        return [(j * CONT, None) for j in range(prompts)] + [
            (pl.multiple_of(PROMPT + c * CONT, CONT), "own")
        ]

    def scores(off, key_off, kind, c):
        s = dot_f32(keys_ref[pl.ds(key_off, CONT), :], q_ref[0, :, pl.ds(off, CONT)])
        if kind == "own":
            bias = bias_ref[pl.ds(pl.multiple_of(c * CONT, CONT), CONT), :]
            s = jnp.where(causal, s + jnp.concatenate([bias, bias], 1), NEG)
        if kind == "prompt":
            ids = key_ids + key_off
            s = jnp.where((ids <= row_ids + off) & (ids >= start_ref[:, off : off + CONT]), s, NEG)
        return s

    def step(ahead, s_ahead, behind, s_behind):
        parts = []
        total = acc = None
        ahead_keys = ahead[1] if ahead else []
        behind_keys = behind[1] if behind else []
        for j in range(max(len(ahead_keys), len(behind_keys))):
            if j < len(ahead_keys):
                s = scores(ahead[0], *ahead_keys[j], ahead[2])
                s_ahead[pl.ds(j * CONT, CONT), :] = s
                parts.append(jnp.max(s.reshape(CONT // 8, 8, CONT), 0))
            if j < len(behind_keys):
                p = jnp.exp(s_behind[pl.ds(j * CONT, CONT), :] - behind[3])
                t = jnp.sum(p.reshape(CONT // 8, 8, CONT), 0)
                o = dot_f32(v_ref[0, :, pl.ds(behind_keys[j][0], CONT)], p.astype(bf16))
                total = t if total is None else total + t
                acc = o if acc is None else acc + o
        if behind:
            off, top = behind[0], behind[3]
            total = jnp.sum(total, 0, keepdims=True)
            out = acc / total
            wide_ref[0, :, pl.ds(off, CONT)] = out
            o_ref[0, :, pl.ds(off, CONT)] = out.astype(bf16)
            lse_ref[0, :, pl.ds(off, CONT)] = top + jnp.log(total)
        if ahead:
            top = parts[0]
            for x in parts[1:]:
                top = jnp.maximum(top, x)
            return jnp.max(top, 0, keepdims=True)

    def cont(c):
        return pl.multiple_of(PROMPT + c * CONT, CONT), cont_keys(c), c

    def pair(i, top):
        c = 2 * i
        top1 = step(cont(c + 1), sb_ref, (*cont(c), top), sa_ref)
        return step(cont(c + 2), sa_ref, (*cont(c + 1), top1), sb_ref)

    top = step(cont(0), sa_ref, None, None)
    top = lax.fori_loop(0, CONTS // 2 - 1, pair, top)
    c = CONTS - 2
    top1 = step(cont(c + 1), sb_ref, (*cont(c), top), sa_ref)
    behind, refs = (*cont(c + 1), top1), (sb_ref, sa_ref)
    for i in reversed(range(prompts)):
        off = i * CONT
        keys = [(k, "prompt") for k in range(max(0, off - DOC_MAX), off + CONT, CONT)]
        top = step((off, keys, 0), refs[1], behind, refs[0])
        behind, refs = (off, keys, 0, top), refs[::-1]
    step(None, None, behind, refs[0])


def head_spec(row):
    return pl.BlockSpec((1, HD, GLEN), lambda i: (row, 0, 0))


def whole(*shape):
    return pl.BlockSpec(shape, lambda i: (0,) * len(shape))


def attn_fwd(head, qkv, doc_start, key_bias):
    heads = qkv.shape[0] // 3
    return pl.pallas_call(
        fwd_kernel,
        grid=(1,),
        in_specs=[
            head_spec(head),
            head_spec(head + heads),
            head_spec(head + 2 * heads),
            whole(1, PROMPT),
            whole(GLEN - PROMPT, 128),
        ],
        out_specs=[whole(1, HD, GLEN), whole(1, HD, GLEN), whole(1, 1, GLEN)],
        out_shape=[
            jax.ShapeDtypeStruct((1, HD, GLEN), bf16),
            jax.ShapeDtypeStruct((1, HD, GLEN), f32),
            jax.ShapeDtypeStruct((1, 1, GLEN), f32),
        ],
        scratch_shapes=[
            pltpu.VMEM((GLEN, HD), bf16),
            pltpu.VMEM((PROMPT + CONT, CONT), f32),
            pltpu.VMEM((PROMPT + CONT, CONT), f32),
        ],
        cost_estimate=pl.CostEstimate(flops=17_000_000_000, transcendentals=0, bytes_accessed=4_000_000),
        name="attn_fwd",
    )(qkv, qkv, qkv, doc_start, key_bias)


SMEM_SPEC = pl.BlockSpec(memory_space=pltpu.SMEM)
KEYS = 512
SPAN = 1024


def bwd_kernel(
    last_ref, slots_ref, q_ref, k_ref, v_ref, g0, g1, g2, g3, wide_ref, lse_ref, start_ref, bias_ref,
    out_ref, qn, kn, vn, gn, qx, gx, dq,
):
    qn[...] = q_ref[0].T
    for n, piece in enumerate((g0, g1, g2, g3)):
        size = piece.shape[1]
        place = pl.ds(pl.multiple_of(slots_ref[n] * size, size), size)
        gx[0:HD, place] = piece[...]
        gn[place, :] = piece[...].T
    ones = jnp.where(lax.broadcasted_iota(jnp.int32, (GLEN, HD), 1) < 3, 1.0, 0.0).astype(bf16)
    kn[:, :HD] = k_ref[0].T
    kn[:, HD:] = ones
    vn[:, :HD] = v_ref[0].T
    vn[:, HD:] = ones
    zeros = jnp.zeros((HD - 16, GLEN), bf16)
    row = lax.broadcasted_iota(jnp.int32, (16, GLEN), 0)

    def extend(ref, tail):
        a, b, c = (jnp.broadcast_to(x.astype(f32), (16, GLEN)) for x in split3(-tail))
        ref[HD : HD + 16, :] = jnp.where(
            row == 0, a, jnp.where(row == 1, b, jnp.where(row == 2, c, 0.0))
        ).astype(bf16)
        ref[HD + 16 :, :] = zeros

    qx[0:HD, :] = q_ref[0]
    extend(qx, lse_ref[0])
    extend(gx, jnp.sum(gx[0:HD, :].astype(f32) * wide_ref[0], 0, keepdims=True))
    dq[...] = jnp.zeros_like(dq)

    def block(key_off, key_span, off, span, mask):
        rows = pl.ds(off, span)
        keys = pl.ds(key_off, key_span)
        s = dot_f32(kn[keys, :], qx[:, rows])
        if mask is not None:
            s = mask(s)
        p = jnp.exp(s)
        ds = (p * dot_f32(vn[keys, :], gx[:, rows])).astype(bf16)
        dv = dot_f32(p.astype(bf16), gn[rows, :])
        dk = dot_f32(ds, qn[rows, :])
        dq[:, rows] += dot_f32(k_ref[0, :, keys], ds)
        return dk, dv

    def emit(key_off, key_span, dk, dv):
        out_ref[1, :, pl.ds(key_off, key_span)] = dk.T.astype(bf16)
        out_ref[2, :, pl.ds(key_off, key_span)] = dv.T.astype(bf16)

    def key_block(b, carry):
        key_off = pl.multiple_of(b * KEYS, KEYS)

        def continuation(c, acc):
            off = pl.multiple_of(PROMPT + c * SPAN, SPAN)
            dk, dv = block(key_off, KEYS, off, SPAN, None)
            return acc[0] + dk, acc[1] + dv

        zero = jnp.zeros((KEYS, HD), f32)
        acc = lax.fori_loop(0, (GLEN - PROMPT) // SPAN, continuation, (zero, zero))

        def prompt(i, acc):
            off = pl.multiple_of(i * CONT, CONT)

            def mask(s):
                key_ids = key_off + lax.broadcasted_iota(jnp.int32, s.shape, 0)
                row_ids = off + lax.broadcasted_iota(jnp.int32, s.shape, 1)
                keep = (key_ids <= row_ids) & (key_ids >= start_ref[:, pl.ds(off, CONT)])
                return jnp.where(keep, s, NEG)

            dk, dv = block(key_off, KEYS, off, CONT, mask)
            return acc[0] + dk, acc[1] + dv

        first = key_off // CONT
        acc = lax.fori_loop(first, last_ref[first + KEYS // CONT - 1], prompt, acc)
        emit(key_off, KEYS, *acc)
        return carry

    lax.fori_loop(0, PROMPT // KEYS, key_block, 0)
    causal = lax.broadcasted_iota(jnp.int32, (CONT, CONT), 0) <= lax.broadcasted_iota(
        jnp.int32, (CONT, CONT), 1
    )

    def own(c, carry):
        off = pl.multiple_of(PROMPT + c * CONT, CONT)
        bias = bias_ref[pl.ds(pl.multiple_of(c * CONT, CONT), CONT), :]

        def mask(s):
            return jnp.where(causal, s + jnp.concatenate([bias, bias], 1), NEG)

        emit(off, CONT, *block(off, CONT, off, CONT, mask))
        return carry

    lax.fori_loop(0, CONTS, own, 0)
    out_ref[0] = (dq[...] * SCALE).astype(bf16)


def attn_bwd(head, grads, bounds, slots, qkv, pieces, row, wide, lse, doc_start, key_bias):
    heads = qkv.shape[0] // 3
    specs = [
        SMEM_SPEC,
        SMEM_SPEC,
        head_spec(head),
        head_spec(head + heads),
        head_spec(head + 2 * heads),
    ]
    specs += [pl.BlockSpec((HD, piece.shape[1]), lambda i: (row, 0)) for piece in pieces]
    specs += [
        whole(1, HD, GLEN),
        whole(1, 1, GLEN),
        whole(1, PROMPT),
        whole(GLEN - PROMPT, 128),
    ]
    args = [bounds, slots, qkv, qkv, qkv, *pieces, wide, lse, doc_start, key_bias]
    kernel = bwd_kernel
    aliases = {}
    if grads is not None:
        specs.append(pl.BlockSpec(memory_space=pl.ANY))
        aliases = {len(args): 0}
        args.append(grads)
        kernel = lambda *refs: bwd_kernel(*refs[:13], *refs[14:])
    return pl.pallas_call(
        kernel,
        grid=(1,),
        in_specs=specs,
        out_specs=pl.BlockSpec((3, None, HD, GLEN), lambda i: (0, head, 0, 0)),
        out_shape=jax.ShapeDtypeStruct((3, heads, HD, GLEN), bf16),
        scratch_shapes=[
            pltpu.VMEM((GLEN, HD), bf16),
            pltpu.VMEM((GLEN, 2 * HD), bf16),
            pltpu.VMEM((GLEN, 2 * HD), bf16),
            pltpu.VMEM((GLEN, HD), bf16),
            pltpu.VMEM((2 * HD, GLEN), bf16),
            pltpu.VMEM((2 * HD, GLEN), bf16),
            pltpu.VMEM((HD, GLEN), f32),
        ],
        input_output_aliases=aliases,
        cost_estimate=pl.CostEstimate(flops=30_000_000_000, transcendentals=0, bytes_accessed=8_000_000),
        name="attn_bwd",
    )(*args)


def normalize(values):
    centred = values - jnp.mean(values, axis=-1, keepdims=True)
    spread = jnp.mean(centred * centred, axis=-1, keepdims=True)
    return centred * lax.rsqrt(spread + norm_eps)


def affine_norm(values, norm_gain, norm_shift):
    return normalize(values) * norm_gain + norm_shift


GELU_C = 0.7978845608028654
GELU_A = 0.044715
BLOCK = 256


def dot(a, b, ca, cb):
    return lax.dot_general(a, b, (((ca,), (cb,)), ((), ())), preferred_element_type=f32)


def row_norm(values):
    centred = values - jnp.mean(values, axis=-1, keepdims=True)
    rstd = lax.rsqrt(jnp.mean(centred * centred, axis=-1, keepdims=True) + norm_eps)
    return centred * rstd, rstd


def norm_pull(norm, rstd, adj):
    first = jnp.mean(adj, axis=-1, keepdims=True)
    second = jnp.mean(adj * norm, axis=-1, keepdims=True)
    return (adj - first - norm * second) * rstd


def join_rows(joined, *parts):
    @pl.when(pl.program_id(0) == 0)
    def _():
        size = parts[0].shape[0]
        for k, part in enumerate(parts):
            joined[k * size : (k + 1) * size, :] = part[...]


def packed_specs(rows):
    once = pl.Buffered(1)
    expand = pl.BlockSpec((D, D), lambda i: (0, 0), pipeline_mode=once)
    reduce = pl.BlockSpec((D, D), lambda i: (1, 0), pipeline_mode=once)
    size = rows - 2 * D
    last = pl.BlockSpec((size, D), lambda i: (2 * D // size, 0), pipeline_mode=once)
    return [expand] * 4 + [reduce] * 4 + [last] * 4


def mid_fwd_kernel(
    scale_ref, a0, a1, a2, a3, b0, b1, b2, b3,
    x_ref, embed_ref, gain_ref, shift_ref, teacher_ref, cot_ref, valid_ref,
    e0, e1, e2, e3, r0, r1, r2, r3, w0, w1, w2, w3,
    layer_ref, norm_ref, act_ref, slope_ref, branch_ref, middle_ref, adj_ref, att_ref, squares_ref, out_w,
):
    join_rows(out_w, w0, w1, w2, w3)
    place = 0
    for piece in (a0, b0, a1, b1, a2, b2, a3, b3):
        att_ref[place : place + piece.shape[0], :] = piece[...]
        place += piece.shape[0]
    hidden = x_ref[...].astype(f32) + embed_ref[...]
    middle = hidden + dot(att_ref[...], out_w[...], 0, 0)
    middle_ref[...] = middle
    normed = (row_norm(middle)[0] * gain_ref[...] + shift_ref[...]).astype(bf16)
    norm_ref[...] = normed
    total = middle
    for k, (expand, reduce) in enumerate(((e0, r0), (e1, r1), (e2, r2), (e3, r3))):
        u = dot(normed, expand[...], 1, 0)
        square = u * u
        th = jnp.tanh(GELU_C * (u + GELU_A * (u * square)))
        half = 0.5 * (1.0 + th)
        act = (u * half).astype(bf16)
        act_ref[k] = act
        slope_ref[k] = half + (0.5 * GELU_C) * u * (1.0 - th * th) * (1.0 + (3.0 * GELU_A) * square)
        total = total + dot(act, reduce[...], 1, 0)
    layer_ref[...] = total.astype(bf16)
    deviation = valid_ref[...] * (total - teacher_ref[...].astype(f32))
    out_adj = cot_ref[...].astype(f32) + scale_ref[0, 0] * deviation
    adj_ref[...] = out_adj
    branch_ref[...] = out_adj.astype(bf16)

    @pl.when(pl.program_id(0) == 0)
    def _():
        squares_ref[...] = jnp.zeros_like(squares_ref)

    squares_ref[...] += jnp.sum(deviation * deviation, axis=0, keepdims=True)


def mid_bwd_kernel(
    branch_ref, slope_ref, middle_ref, adj_ref, gain_ref, e0, e1, e2, e3, r0, r1, r2, r3, w0, w1, w2, w3,
    pre_ref, middle_adj_ref, attn_ref, att_ref, gain_out, shift_out, out_w,
):
    join_rows(out_w, w0, w1, w2, w3)
    branch = branch_ref[...]
    second = None
    for k, (expand, reduce) in enumerate(((e0, r0), (e1, r1), (e2, r2), (e3, r3))):
        pre = (dot(branch, reduce[...], 1, 1) * slope_ref[k]).astype(bf16)
        pre_ref[k] = pre
        part = dot(pre, expand[...], 1, 1)
        second = part if second is None else second + part
    norm, rstd = row_norm(middle_ref[...])

    @pl.when(pl.program_id(0) == 0)
    def _():
        gain_out[...] = jnp.zeros_like(gain_out)
        shift_out[...] = jnp.zeros_like(shift_out)

    gain_out[...] += jnp.sum(second * norm, axis=0, keepdims=True)
    shift_out[...] += jnp.sum(second, axis=0, keepdims=True)
    middle_adj = adj_ref[...] + norm_pull(norm, rstd, second * gain_ref[...])
    middle_adj_ref[...] = middle_adj
    attn_adj = middle_adj.astype(bf16)
    attn_ref[...] = attn_adj
    att_ref[...] = dot(out_w[...], attn_adj, 1, 1).astype(bf16)


def fixed(shape):
    return pl.BlockSpec(shape, lambda i: (0,) * len(shape), pipeline_mode=pl.Buffered(1))


def by_rows(width):
    return pl.BlockSpec((BLOCK, width), lambda i: (i, 0))


def by_rows4(width):
    return pl.BlockSpec((4, BLOCK, width), lambda i: (0, i, 0))


def by_cols(height):
    return pl.BlockSpec((height, BLOCK), lambda i: (0, i))


def mid_fwd(scale, att, x, embed, gain, shift, teacher, cot, valid, weights):
    rows = x.shape[0]
    width = D
    shape = jax.ShapeDtypeStruct
    return pl.pallas_call(
        mid_fwd_kernel,
        grid=(rows // BLOCK,),
        in_specs=[
            pl.BlockSpec(memory_space=pltpu.SMEM),
        ] + [by_cols(piece.shape[0]) for piece in att] + [
            by_rows(D), fixed((1, D)), fixed((1, D)),
            fixed((1, D)), by_rows(D), by_rows(D), by_rows(1),
        ] + packed_specs(weights[0].shape[0]),
        out_specs=[
            by_rows(D), by_rows(D), by_rows4(width), by_rows4(width), by_rows(D), by_rows(D), by_rows(D),
            by_cols(D), fixed((1, D)),
        ],
        out_shape=[
            shape((rows, D), bf16), shape((rows, D), bf16), shape((4, rows, width), bf16),
            shape((4, rows, width), f32), shape((rows, D), bf16), shape((rows, D), f32),
            shape((rows, D), f32), shape((D, rows), bf16), shape((1, D), f32),
        ],
        cost_estimate=pl.CostEstimate(flops=22_000_000_000, transcendentals=0, bytes_accessed=30_000_000),
        scratch_shapes=[pltpu.VMEM((D, D), bf16)],
        name="mid_fwd",
    )(scale, *att, x, embed, gain, shift, teacher, cot, valid, *weights, *weights, *weights)


def mid_bwd(branch, slope, middle, adj, gain, weights):
    rows = branch.shape[0]
    width = D
    shape = jax.ShapeDtypeStruct
    return pl.pallas_call(
        mid_bwd_kernel,
        grid=(rows // BLOCK,),
        in_specs=[by_rows(D), by_rows4(width), by_rows(D), by_rows(D), fixed((1, D))]
        + packed_specs(weights[0].shape[0]),
        out_specs=[by_rows4(width), by_rows(D), by_rows(D), by_cols(D), fixed((1, D)), fixed((1, D))],
        out_shape=[
            shape((4, rows, width), bf16), shape((rows, D), f32), shape((rows, D), bf16),
            shape((D, rows), bf16), shape((1, D), f32), shape((1, D), f32),
        ],
        cost_estimate=pl.CostEstimate(flops=22_000_000_000, transcendentals=0, bytes_accessed=30_000_000),
        scratch_shapes=[pltpu.VMEM((D, D), bf16)],
        name="mid_bwd",
    )(branch, slope, middle, adj, gain, *weights, *weights, *weights)


def swap(x, bit, axis="tensor"):
    size = lax.axis_size(axis)
    return lax.ppermute(x, axis, [(i, i ^ bit) for i in range(size)])


def sum_small(x, axis):
    for shift, members in levels(axis):
        x = sum((swap(x, j << shift, axis) for j in range(1, members)), x)
    return x


def levels(axis):
    steps, shift, size = [], 0, lax.axis_size(axis)
    while 1 << shift < size:
        members = 2 if shift == 0 or size >> shift < 4 else 4
        steps.append((shift, members))
        shift += members.bit_length() - 1
    return steps


def sum_scatter(x, axis):
    for shift, members in levels(axis):
        digit = (lax.axis_index(axis) >> shift) & (members - 1)
        x = x.reshape(members, x.shape[0] // members, x.shape[1])
        total = lax.dynamic_index_in_dim(x, digit, 0, False)
        for j in range(1, members):
            sent = lax.dynamic_index_in_dim(x, digit ^ j, 0, False).astype(bf16)
            total = total + swap(sent, j << shift, axis).astype(f32)
        x = total
    return x.astype(bf16)


def spread(x, axis):
    for shift, members in reversed(levels(axis)):
        digit = (lax.axis_index(axis) >> shift) & (members - 1)
        parts = [x] + [swap(x, j << shift, axis) for j in range(1, members)]
        rows = []
        for i in range(members):
            row = parts[0]
            for j in range(1, members):
                row = jnp.where(digit ^ j == i, parts[j], row)
            rows.append(row)
        x = jnp.concatenate(rows, 0)
    return x.astype(f32)


def sum_all(x, axis):
    return spread(sum_scatter(x, axis), axis)


def gather4(x):
    far = swap(x, 2)
    near = swap(x, 1)
    return [x, near, far, swap(far, 1)]


def scatter4(parts):
    near3 = swap(parts[3], 1)
    near1 = swap(parts[1], 1)
    across = (parts[2].astype(f32) + near3.astype(f32)).astype(bf16)
    mine = parts[0].astype(f32) + near1.astype(f32)
    return mine + swap(across, 2).astype(f32)


def layer(
    layer_input,
    out_cotangent,
    teacher,
    valid_mask,
    prompt_docs,
    pass_embed,
    first_gain,
    first_shift,
    project_in,
    project_out,
    second_gain,
    second_shift,
    expand_weight,
    reduce_weight,
):
    rows = layer_input.shape[0]
    width = project_out.shape[0]
    heads = width // HD
    t = lax.axis_index("tensor")
    slots = [t ^ k for k in range(4)]
    valid = valid_mask[0]
    docs = prompt_docs[0]
    valid_total = sum_small(jnp.sum(valid).astype(f32).reshape(1, 1), "dp")[0, 0]
    doc_start = jnp.zeros_like(docs)
    for v in range(3):
        doc_start = doc_start + jnp.where(docs > v, jnp.sum((docs == v).astype(jnp.int32)), 0)
    edges = jnp.arange(CONT, PROMPT + 1, CONT, dtype=jnp.int32)
    last_block = (jnp.sum((doc_start[None, :] < edges[:, None]).astype(jnp.int32), 1) + CONT - 1) // CONT
    doc_start = doc_start[None, :]
    key_bias = jnp.broadcast_to(jnp.where(valid == 1, 0.0, NEG).astype(f32)[:, None], (GLEN - PROMPT, 128))
    row_valid = lax.dynamic_slice_in_dim(
        jnp.concatenate([jnp.zeros((PROMPT,), f32), valid.astype(f32)]), t * rows, rows
    )[:, None]

    hidden_in = layer_input.astype(f32) + pass_embed
    first_affine = affine_norm(hidden_in, first_gain, first_shift)
    first_norm = first_affine.astype(bf16)
    far = swap(first_norm, 2)
    near = swap(first_norm, 1)
    in_matrix = project_in.reshape(D, 3 * width)

    def project(block):
        part = dot(in_matrix, block, 0, 1).astype(bf16)
        return jnp.concatenate([part[:width] * SCALE, part[width:]], 0)

    qkv = lax.dynamic_update_slice(jnp.zeros((3 * width, GLEN), bf16), project(first_norm), (0, slots[0] * rows))
    far, valid_total, qkv = lax.optimization_barrier((far, valid_total, qkv))
    divisor = valid_total * D
    first_blocks = [first_norm, near, far, swap(far, 1)]
    packed = jnp.concatenate([expand_weight, reduce_weight, project_out], 0)
    packed, _ = lax.optimization_barrier((packed, far))
    weights = gather4(packed)

    for k in range(1, 4):
        qkv = lax.dynamic_update_slice(qkv, project(first_blocks[k]), (0, slots[k] * rows))
    qkv = qkv.reshape(3 * heads, HD, GLEN)
    saved = []
    for h in range(heads):
        saved.append(attn_fwd(h, qkv, doc_start, key_bias))
    groups = [saved[:-1], saved[-1:]]
    moved = []
    for group in groups:
        att = jnp.concatenate([x[0][0] for x in group], 0)
        cut = lambda k: lax.dynamic_slice(att, (0, slots[k] * rows), (att.shape[0], rows))
        got = {k: swap(cut(k), k) for k in (3, 2, 1)}
        got[0] = cut(0)
        moved.append(got)
    att_pieces = [got[k] for got in moved for k in range(4)]
    layer_out, second_norm, acts, slope, branch_adj, middle, out_adj, att_own, squares = mid_fwd(
        (2.0 / divisor).reshape(1, 1), att_pieces, layer_input, pass_embed[None], second_gain[None],
        second_shift[None], teacher, out_cotangent, row_valid, weights,
    )
    reduce_parts = [dot(acts[k], branch_adj, 0, 0).astype(bf16) for k in range(4)]
    branch_adj, *reduce_parts = lax.optimization_barrier((branch_adj, *reduce_parts))
    reduce_grad = sum_all(scatter4(reduce_parts), "dp")
    pre_adjs, middle_adj, attn_adj, att_adj, second_gain_part, second_shift_part = mid_bwd(
        branch_adj, slope, middle, out_adj, second_gain[None], weights
    )
    att_adj = att_adj.reshape(4, heads, HD, rows)
    adj_heads = []
    for first, last in ((0, 1), (1, heads)):
        pieces = [None] * 4
        for k in (3, 2, 1, 0):
            piece = att_adj[k, first:last].reshape((last - first) * HD, rows)
            pieces[k] = swap(piece, k) if k else piece
        adj_heads += [(pieces, h) for h in range(last - first)]

    expand_parts = [dot(second_norm, pre_adjs[k], 0, 0).astype(bf16) for k in range(4)]
    out_parts = dot(att_own, attn_adj, 1, 0).astype(bf16)
    other_parts = [
        jnp.concatenate([expand_parts[k], out_parts[k * width : (k + 1) * width]], 0) for k in range(4)
    ]
    own, *other_parts = lax.optimization_barrier((adj_heads[0][0][0], *other_parts))
    adj_heads[0][0][0] = own
    other_grad = sum_all(scatter4(other_parts), "dp")

    proj_adj = None
    for h in range(heads):
        proj_adj = attn_bwd(h, proj_adj, last_block, jnp.stack(slots), qkv, *adj_heads[h], *saved[h][1:], doc_start, key_bias)
    proj_adj = proj_adj.reshape(3 * width, GLEN)
    spare = -(3 * width) % (16 * lax.axis_size("dp"))

    def part(k):
        piece = lax.dynamic_slice(proj_adj, (0, slots[k] * rows), (3 * width, rows))
        return dot(in_matrix, piece, 1, 0).astype(bf16)

    near3 = swap(part(3), 1)
    across = (part(2).astype(f32) + near3.astype(f32)).astype(bf16)
    far = swap(across, 2)
    order = (1, 0, 3, 2)
    part1, part0, gained = tail(
        jnp.stack([slots[k] for k in order]), proj_adj, in_matrix, [first_blocks[k] for k in order], spare
    )
    near1 = swap(part1, 1)
    in_proj_grad = sum_all(gained, "dp")[: 3 * width]
    input_gradient, embed_part, first_gain_part, first_shift_part = final(
        layer_input, pass_embed[None], first_gain[None], part0, near1, far, middle_adj
    )
    small = jnp.stack(
        [
            embed_part[0],
            first_gain_part[0],
            first_shift_part[0],
            second_gain_part[0],
            second_shift_part[0],
            squares[0],
        ]
    )
    small = sum_small(sum_small(small, "tensor"), "dp")
    return (
        layer_out,
        jnp.sum(small[5]) / divisor,
        input_gradient,
        small[0],
        small[1],
        small[2],
        in_proj_grad.reshape(3, width, D).transpose(2, 0, 1),
        other_grad[D:],
        small[3],
        small[4],
        other_grad[:D],
        reduce_grad,
    )


def tail_kernel(slots_ref, grads, weight, x0, x1, x2, x3, fa, fb, sum_ref):
    step = pl.program_id(0)
    width = grads.shape[0]
    for k, x in enumerate((x0, x1, x2, x3)):

        @pl.when(step == k)
        def _():
            gained = dot_f32(grads[...], x[...])
            if k == 0:
                sum_ref[:width, :] = gained
                sum_ref[width:, :] = jnp.zeros((sum_ref.shape[0] - width, D), f32)
            else:
                sum_ref[:width, :] += gained
            if k < 2:
                (fa, fb)[k][...] = dot_f32(weight[...], grads[...]).astype(bf16)


def tail(slots, grads, weight, blocks, spare):
    width, rows = grads.shape[0], blocks[0].shape[0]
    once = lambda *shape: pl.BlockSpec(shape, lambda i, s: (0, 0), pipeline_mode=pl.Buffered(1))
    return pl.pallas_call(
        tail_kernel,
        grid_spec=pltpu.PrefetchScalarGridSpec(
            num_scalar_prefetch=1,
            grid=(4,),
            in_specs=[pl.BlockSpec((width, rows), lambda i, s: (0, s[i])), once(D, width)] + [once(rows, D)] * 4,
            out_specs=[once(D, rows), once(D, rows), once(width + spare, D)],
        ),
        out_shape=[jax.ShapeDtypeStruct((D, rows), bf16)] * 2 + [jax.ShapeDtypeStruct((width + spare, D), f32)],
        cost_estimate=pl.CostEstimate(flops=14_000_000_000, transcendentals=0, bytes_accessed=12_000_000),
        name="tail",
    )(slots, grads, weight, *blocks)


def final_kernel(
    x_ref, embed_ref, gain_ref, part_ref, near_ref, far_ref, adj_ref, out_ref, embed_out, gain_out, shift_out
):
    norm, rstd = row_norm(x_ref[...].astype(f32) + embed_ref[...])
    first = (part_ref[...].astype(f32) + near_ref[...].astype(f32) + far_ref[...].astype(f32)).T
    input_adj = adj_ref[...] + norm_pull(norm, rstd, first * gain_ref[...])
    out_ref[...] = input_adj.astype(bf16)

    @pl.when(pl.program_id(0) == 0)
    def _():
        embed_out[...] = jnp.zeros_like(embed_out)
        gain_out[...] = jnp.zeros_like(gain_out)
        shift_out[...] = jnp.zeros_like(shift_out)

    embed_out[...] += jnp.sum(input_adj, axis=0, keepdims=True)
    gain_out[...] += jnp.sum(first * norm, axis=0, keepdims=True)
    shift_out[...] += jnp.sum(first, axis=0, keepdims=True)


def final(x, embed, gain, part, near, far, adj):
    rows = x.shape[0]
    line = jax.ShapeDtypeStruct((1, D), f32)
    return pl.pallas_call(
        final_kernel,
        grid=(rows // BLOCK,),
        in_specs=[by_rows(D), fixed((1, D)), fixed((1, D))] + [by_cols(D)] * 3 + [by_rows(D)],
        out_specs=[by_rows(D)] + [fixed((1, D))] * 3,
        out_shape=[jax.ShapeDtypeStruct((rows, D), bf16), line, line, line],
        name="final",
    )(x, embed, gain, part, near, far, adj)


def solution(mesh):
    rows = P(("dp", "tensor"), None)
    return jax.shard_map(
        layer,
        mesh=mesh,
        in_specs=(
            rows,
            rows,
            rows,
            P("dp", None),
            P("dp", None),
            P(),
            P(),
            P(),
            P(None, None, "tensor"),
            P("tensor", None),
            P(),
            P(),
            P(None, "tensor"),
            P("tensor", None),
        ),
        out_specs=(
            rows,
            P(),
            rows,
            P(),
            P(),
            P(),
            P(None, None, "tensor"),
            P("tensor", None),
            P(),
            P(),
            P(None, "tensor"),
            P("tensor", None),
        ),
        check_vma=False,
    )
```
